32 devices in a mesh: enc: 8 (over z, y), slide: 4 (over x, core).
Axes of the slice: x: 2, y: 2, z: 4, core: 2. Of those that a mesh axis runs over, the one named last changes fastest.
Arguments:
- tile_features: bfloat16 [512, 7, 7, 768], P(('enc', 'slide')), may hold values from -6 to 6
- tile_slide: int32 [512, 1], P(('enc', 'slide')), may hold values from 0 to 7, as said below
- slide_order: int32 [8, 8], P('enc'), may hold values from 0 to 7, each once within a row
- targets: float32 [8, 8, 256], P('enc', 'slide'), may hold values from -6 to 6
- dw_kernel: bfloat16 [49, 768], replicated, may hold values from -0.875 to 0.875
- dw_bias: bfloat16 [768], replicated, may hold values from -3 to 3
- norm_gain: bfloat16 [768], replicated, may hold values from 0.25 to 1.75
- norm_bias: bfloat16 [768], replicated, may hold values from -3 to 3
- w_in: bfloat16 [3072, 768], replicated, may hold values from -0.21875 to 0.21875
- in_bias: bfloat16 [3072], replicated, may hold values from -3 to 3
- w_out: bfloat16 [3072, 768], replicated, may hold values from -0.109375 to 0.109375
- out_bias: bfloat16 [768], replicated, may hold values from -3 to 3
- layer_scale: bfloat16 [768], replicated, may hold values from 0.19921875 to 2
- final_gain: bfloat16 [768], replicated, may hold values from 0.25 to 1.75
- final_bias: bfloat16 [768], replicated, may hold values from -3 to 3
- head_weight: bfloat16 [768, 256], replicated, may hold values from -0.21875 to 0.21875
- head_bias: bfloat16 [256], replicated, may hold values from -3 to 3
Outputs:
- grad_w_in: float32 [3072, 768], P(('enc', 'slide'))
- grad_w_out: float32 [3072, 768], P(('enc', 'slide'))
- grad_dw_kernel: float32 [49, 768], replicated
- grad_vectors: float32 [7, 768], replicated
- grad_in_bias: float32 [3072], replicated
- grad_head_weight: float32 [768, 256], replicated
- grad_head_bias: float32 [256], replicated
- slide_loss: float32 [8, 8], P('enc', 'slide')
The draws below stay inside these ranges and needn't reach their ends.
Inputs may be any that keep to these rules, and one draw needn't show every extreme that they name: `tile_slide`: the 16 tiles of one device are the rows of one aligned block; at most 3 tiles of one device belong to one slide, and every device has exactly 3 tiles of some slide; a slide may have no tiles in its group. `slide_order`: each row names every slide number of its group once.
All inputs are finite; a program needn't handle non-finite values.
Results may differ from the reference program's by a relative error of at most 0.0041.
Values may be sent and summed in bfloat16 or wider, within the bound.
A program may use at most 192 MiB of HBM per device.

```python
import math
from functools import partial
import jax
import jax.numpy as jnp
from jax import lax

D = 768
FF = 3072
KERNEL = 7
SIDE = 7
GENES = 256
TILE_DEV = 16
SLIDES_GRP = 8
CAP = 3
TILES = 512
N_ENC = 8
N_SLIDE = 4


def draw_tile_features(key, part):
    keys = jax.random.split(jax.random.fold_in(key, 23), 4)
    tile_scale = jnp.exp(jax.random.uniform(keys[0], (TILES, 1, 1, 1), jnp.float32, -2.0, 1.0))
    channel_scale = jnp.exp(jax.random.uniform(keys[1], (TILES, 1, 1, D), jnp.float32, -0.7, 0.7))
    offset = 0.5 * jax.random.normal(keys[2], (TILES, 1, 1, D), jnp.float32)
    noise = jax.random.normal(keys[3], (TILES, SIDE, SIDE, D), jnp.float32)
    values = tile_scale * (offset + channel_scale * noise)
    return jnp.clip(values, -6.0, 6.0).astype(jnp.bfloat16)


def draw_tile_slide(key, part):
    slots = SLIDES_GRP * CAP
    blocks = N_ENC * N_SLIDE
    keys = jax.random.split(jax.random.fold_in(key, 11), 7)
    forced_group = jax.random.randint(keys[0], (), 0, N_ENC)
    group_ids = jnp.arange(N_ENC, dtype=jnp.int32)
    dropping = (jax.random.randint(keys[1], (N_ENC,), 0, 4) == 0) | (group_ids == forced_group)
    missing = jax.random.randint(keys[2], (N_ENC,), 0, SLIDES_GRP)
    missing = jnp.where(dropping, missing, -1)
    heat = jax.random.randint(keys[3], (N_ENC, SLIDES_GRP), 0, 4)
    block_group = jnp.arange(blocks, dtype=jnp.int32) // N_SLIDE
    block_missing = missing[block_group]
    block_heat = heat[block_group]
    has_missing = block_missing >= 0
    upper = jnp.where(has_missing, SLIDES_GRP - 1, SLIDES_GRP)
    picked = jax.random.randint(keys[4], (blocks,), 0, upper)
    filled = picked + (has_missing & (picked >= block_missing)).astype(jnp.int32)
    slot_ids = jnp.arange(slots, dtype=jnp.int32)
    slot_slide = slot_ids // CAP
    slot_copy = slot_ids % CAP
    noise = jax.random.randint(keys[5], (blocks, slots), 0, 4096)
    penalty = slot_copy[None, :] * (4 - block_heat[:, slot_slide]) * 1024
    score = (noise + penalty) * slots + slot_ids[None, :]
    score = jnp.where(slot_slide[None, :] == filled[:, None], slot_ids[None, :] - 2 * slots, score)
    score = jnp.where(slot_slide[None, :] == block_missing[:, None], 2 ** 30 + slot_ids[None, :], score)
    unused_values, chosen = lax.top_k(-score, TILE_DEV)
    chosen_slide = slot_slide[chosen]
    order_score = jax.random.randint(keys[6], (blocks, TILE_DEV), 0, 2 ** 20) * TILE_DEV + jnp.arange(TILE_DEV, dtype=jnp.int32)[None, :]
    order = jnp.argsort(order_score, axis=1, stable=True)
    shuffled = jnp.take_along_axis(chosen_slide, order, axis=1)
    return shuffled.reshape(blocks * TILE_DEV, 1).astype(jnp.int32)


def block_scale(stream_key, dims, pieces, smallest, high):
    factor_of = 1.0
    for position, parts in pieces:
        draws = jax.random.uniform(jax.random.fold_in(jax.random.fold_in(stream_key, 6), position), (parts,), jnp.float32, smallest / len(pieces), high / len(pieces))
        factor_of = factor_of * jnp.repeat(jnp.exp(draws), dims[position] // parts).reshape((-1,) + (1,) * (len(dims) - 1 - position))
    return factor_of


def normal_values(stream_key, extent, scale, limit, shards=(), kind=jnp.bfloat16):
    array = jax.random.normal(stream_key, extent, jnp.float32) * scale
    if len(shards) > 0:
        array = block_scale(stream_key, extent, shards, -0.22, 0.18) * array
    return jnp.clip(array, min=-limit, max=limit).astype(kind)


def setup_inputs(seed: int = 0) -> dict:
    key_of = jax.random.split(jax.random.key(seed), 18)
    return {
        "tile_features": draw_tile_features(jax.random.fold_in(key_of[17], 71), 0),
        "tile_slide": draw_tile_slide(jax.random.fold_in(key_of[17], 71), 0),
        "slide_order": jax.vmap(lambda own: jax.random.permutation(own, SLIDES_GRP))(jax.random.split(key_of[2], N_ENC)).reshape((N_ENC, SLIDES_GRP)).astype(jnp.int32),
        "targets": normal_values(key_of[3], (N_ENC, SLIDES_GRP, GENES), 1.0, 6.0, ((0, 8), (1, 4)), jnp.float32),
        "dw_kernel": normal_values(key_of[4], (KERNEL * KERNEL, D), (KERNEL * KERNEL) ** -0.5, 0.875),
        "dw_bias": normal_values(key_of[5], (D,), 0.5, 3.0),
        "norm_gain": jnp.clip(1.0 + 0.15 * jax.random.normal(key_of[6], (D,), jnp.float32), 0.25, 1.75).astype(jnp.bfloat16),
        "norm_bias": normal_values(key_of[7], (D,), 0.5, 3.0),
        "w_in": normal_values(key_of[8], (FF, D), D ** -0.5, 0.21875),
        "in_bias": normal_values(key_of[9], (FF,), 0.5, 3.0),
        "w_out": normal_values(key_of[10], (FF, D), FF ** -0.5, 0.109375),
        "out_bias": normal_values(key_of[11], (D,), 0.5, 3.0),
        "layer_scale": jnp.clip(jnp.exp(jax.random.uniform(key_of[12], (D,), jnp.float32, math.log(0.19921875), math.log(2.0))), 0.19921875, 2.0).astype(jnp.bfloat16),
        "final_gain": jnp.clip(1.0 + 0.15 * jax.random.normal(key_of[13], (D,), jnp.float32), 0.25, 1.75).astype(jnp.bfloat16),
        "final_bias": normal_values(key_of[14], (D,), 0.5, 3.0),
        "head_weight": normal_values(key_of[15], (D, GENES), D ** -0.5, 0.21875),
        "head_bias": normal_values(key_of[16], (GENES,), 0.5, 3.0),
    }


epsilon = 1e-06

def layer_norm(values, gain, shift):
    center = values - lax.optimization_barrier(jnp.mean(values, axis=-1, keepdims=True))
    spread = lax.optimization_barrier(jnp.mean(center * center, axis=-1, keepdims=True))
    return center * lax.rsqrt(spread + epsilon) * gain + shift

def depthwise(features, kernel, bias):
    margin = KERNEL // 2
    padded = jnp.pad(features.astype(jnp.float32), ((0, 0), (margin, margin), (margin, margin), (0, 0)))
    total = jnp.zeros(features.shape, jnp.float32) + bias
    for vertical in range(KERNEL):
        for across in range(KERNEL):
            total = total + padded[:, vertical:vertical + SIDE, across:across + SIDE, :] * kernel[vertical * KERNEL + across]
    return total

def prepare_tile(features, kernel, dw_bias, norm_gain, norm_bias):
    conv = depthwise(features, kernel, dw_bias)
    return layer_norm(conv, norm_gain, norm_bias).reshape(-1, features.shape[-1])

def finish_tile(projected, out_bias, layer_scale, final_gain, final_bias, features):
    tile_count = features.shape[0]
    channels = features.shape[-1]
    branch = (projected + out_bias).reshape(tile_count, -1, channels)
    summed = features.astype(jnp.float32).reshape(tile_count, -1, channels) + layer_scale * branch
    pooled = lax.optimization_barrier(jnp.mean(summed, axis=1))
    return layer_norm(pooled, final_gain, final_bias)

def contract_rows(left, right):
    return lax.dot_general(left, right, (((0,), (0,)), ((), ())), preferred_element_type=jnp.float32)

def encode(features, vector_params, w_in, inner_bias, w_out):
    kernel, dw_bias, norm_gain, norm_bias, out_bias, layer_scale, final_gain, final_bias = vector_params
    normed = prepare_tile(features, kernel, dw_bias, norm_gain, norm_bias).astype(jnp.bfloat16)
    hidden = lax.dot_general(normed, w_in, (((1,), (1,)), ((), ())), preferred_element_type=jnp.float32) + inner_bias
    active = jax.nn.gelu(hidden, approximate=False).astype(jnp.bfloat16)
    projected = jnp.dot(active, w_out, preferred_element_type=jnp.float32)
    embedded = finish_tile(projected, out_bias, layer_scale, final_gain, final_bias, features).astype(jnp.bfloat16)
    return (embedded, (normed, hidden, active, projected))

def decode(features, vector_params, w_in, w_out, stored, grad_embed):
    kernel, dw_bias, norm_gain, norm_bias, out_bias, layer_scale, final_gain, final_bias = vector_params
    normed, hidden, active, projected = stored
    unused, pull_finish = jax.vjp(partial(finish_tile, features=features), projected, out_bias, layer_scale, final_gain, final_bias)
    grad_proj, grad_out_bias, grad_scale, grad_fgain, grad_fbias = pull_finish(grad_embed.astype(jnp.float32))
    grad_projected = grad_proj.astype(jnp.bfloat16)
    grad_active = lax.dot_general(grad_projected, w_out, (((1,), (1,)), ((), ())), preferred_element_type=jnp.float32)
    unused_gelu, pull_gelu = jax.vjp(partial(jax.nn.gelu, approximate=False), hidden)
    grad_wide = pull_gelu(grad_active)[0]
    grad_hidden = grad_wide.astype(jnp.bfloat16)
    grad_normed = jnp.dot(grad_hidden, w_in, preferred_element_type=jnp.float32)
    unused_prep, pull_prepare = jax.vjp(partial(prepare_tile, features), kernel, dw_bias, norm_gain, norm_bias)
    grad_kernel, grad_dw_bias, grad_ngain, grad_nbias = pull_prepare(grad_normed)
    vectors = jnp.stack([grad_dw_bias, grad_ngain, grad_nbias, grad_out_bias, grad_scale, grad_fgain, grad_fbias])
    return (grad_projected, grad_hidden, grad_kernel, vectors, lax.optimization_barrier(jnp.sum(grad_wide, axis=0)))

def reference(tile_features, tile_slide, slide_order, targets, dw_kernel, dw_bias, norm_gain, norm_bias, w_in, in_bias, w_out, out_bias, layer_scale, final_gain, final_bias, head_weight, head_bias):
    highest = lax.Precision.HIGHEST
    blocks = N_ENC * N_SLIDE
    group_tiles = N_SLIDE * TILE_DEV
    vector_params = tuple((param.astype(jnp.float32) for param in (dw_kernel, dw_bias, norm_gain, norm_bias, out_bias, layer_scale, final_gain, final_bias)))
    inner_bias = in_bias.astype(jnp.float32)
    features_all = tile_features.reshape(blocks, TILE_DEV, SIDE, SIDE, D)

    def forward_block(features):
        return encode(features, vector_params, w_in, inner_bias, w_out)[0]
    embedded = lax.map(forward_block, features_all).reshape(N_ENC, group_tiles, D)
    slide_ids = tile_slide[:, 0].reshape(N_ENC, group_tiles)
    numbers = jnp.arange(SLIDES_GRP, dtype=jnp.int32)
    tile_hot = (slide_ids[:, None, :] == numbers[None, :, None]).astype(jnp.float32)
    id_sums = jnp.einsum('ekt,etd->ekd', tile_hot, embedded.astype(jnp.float32), precision=highest)
    id_counts = lax.optimization_barrier(jnp.sum(tile_hot, axis=2))
    order_hot = (slide_order[:, :, None] == numbers[None, None, :]).astype(jnp.float32)
    slide_sums = jnp.einsum('epk,ekd->epd', order_hot, id_sums, precision=highest)
    slide_counts = jnp.einsum('epk,ek->ep', order_hot, id_counts, precision=highest)
    divisor = jnp.maximum(slide_counts, 1.0)[:, :, None]
    slide_mean = slide_sums / divisor
    head_wide = head_weight.astype(jnp.float32)
    prediction = jnp.einsum('epd,dg->epg', slide_mean, head_wide, precision=highest) + head_bias.astype(jnp.float32)
    difference = prediction - targets
    slide_loss = 0.5 * lax.optimization_barrier(jnp.mean(difference * difference, axis=-1))
    grad_pred = difference / GENES
    grad_head_w = jnp.einsum('epd,epg->dg', slide_mean, grad_pred, precision=highest)
    grad_head_b = lax.optimization_barrier(jnp.sum(grad_pred, axis=(0, 1)))
    grad_mean = jnp.einsum('epg,dg->epd', grad_pred, head_wide, precision=highest)
    slide_grad = (grad_mean / divisor).astype(jnp.bfloat16)
    id_grad = jnp.einsum('epk,epd->ekd', order_hot, slide_grad.astype(jnp.float32), precision=highest)
    grad_embed = jnp.einsum('ekt,ekd->etd', tile_hot, id_grad, precision=highest).astype(jnp.bfloat16).reshape(blocks, TILE_DEV, D)

    def accumulate(running, block):
        features, grad_block = block
        unused, stored = encode(features, vector_params, w_in, inner_bias, w_out)
        grad_projected, grad_hidden, grad_kernel, grad_vectors, grad_inner = decode(features, vector_params, w_in, w_out, stored, grad_block)
        normed, hidden, active, projected = stored
        terms = (contract_rows(grad_hidden, normed), contract_rows(active, grad_projected), grad_kernel, grad_vectors, grad_inner)
        return (jax.tree.map(jnp.add, running, terms), None)
    initial = (jnp.zeros((FF, D), jnp.float32), jnp.zeros((FF, D), jnp.float32), jnp.zeros((KERNEL * KERNEL, D), jnp.float32), jnp.zeros((7, D), jnp.float32), jnp.zeros((FF,), jnp.float32))
    totals, unused_ys = lax.scan(accumulate, initial, (features_all, grad_embed))
    return (totals[0], totals[1], totals[2], totals[3], totals[4], grad_head_w, grad_head_b, slide_loss)
```

```python
import math
from functools import partial

import jax
import jax.numpy as jnp
from jax import lax
from jax.experimental import pallas as pl
from jax.experimental.pallas import tpu as pltpu
from jax.sharding import PartitionSpec as P

KERNEL = 7
SIDE = 7
MARGIN = KERNEL // 2
POSITIONS = SIDE * SIDE
LANES = 128
EPSILON = 1e-06
VMEM_LIMIT = 56 * 1024 * 1024
AXES = ("enc", "slide")


def layer_norm(values, gain, shift):
    center = values - jnp.mean(values, axis=-1, keepdims=True)
    spread = jnp.mean(center * center, axis=-1, keepdims=True)
    return center * lax.rsqrt(spread + EPSILON) * gain + shift


def whole_vmem(count):
    return [pl.BlockSpec(memory_space=pltpu.VMEM)] * count


def prepare_kernel(x_ref, k_ref, bias_ref, gain_ref, shift_ref, normed_ref, hat_ref, rstd_ref, fsum_ref, xs, ks):
    tiles, channels = x_ref.shape[1], x_ref.shape[2]
    ks[...] = k_ref[...].astype(jnp.float32)

    def block(c, carry):
        lanes = pl.ds(pl.multiple_of(c * LANES, LANES), LANES)
        total = jnp.zeros((tiles, LANES), jnp.float32)
        for p in range(POSITIONS):
            value = x_ref[p, :, lanes].astype(jnp.float32)
            xs[p] = value
            total = total + value
        fsum_ref[:, lanes] = total
        bias = jnp.broadcast_to(bias_ref[:, lanes].astype(jnp.float32), (tiles, LANES))
        for i in range(SIDE):
            accs = [bias for _ in range(SIDE)]
            for a in range(KERNEL):
                row = i + a - MARGIN
                if row < 0 or row >= SIDE:
                    continue
                weights = [ks[pl.ds(a * KERNEL + b, 1), lanes] for b in range(KERNEL)]
                for col in range(SIDE):
                    value = xs[row * SIDE + col]
                    for j in range(SIDE):
                        b = col - j + MARGIN
                        if 0 <= b < KERNEL:
                            accs[j] = accs[j] + value * weights[b]
            for j in range(SIDE):
                rows = pl.ds((i * SIDE + j) * tiles, tiles)
                hat_ref[rows, lanes] = accs[j]
        return carry

    lax.fori_loop(0, channels // LANES, block, 0)
    gain = gain_ref[...].astype(jnp.float32)
    shift = shift_ref[...].astype(jnp.float32)

    def norm(p, carry):
        rows = pl.ds(pl.multiple_of(p * tiles, tiles), tiles)
        conv = hat_ref[rows, :]
        center = conv - jnp.mean(conv, axis=-1, keepdims=True)
        spread = jnp.mean(center * center, axis=-1, keepdims=True)
        rstd = lax.rsqrt(spread + EPSILON)
        hat = center * rstd
        hat_ref[rows, :] = hat
        normed_ref[rows, :] = (hat * gain + shift).astype(jnp.bfloat16)
        rstd_ref[rows, :] = jnp.broadcast_to(rstd, (tiles, LANES))
        return carry

    lax.fori_loop(0, POSITIONS, norm, 0, unroll=7)


def prepare(x, kernel, bias, gain, shift):
    positions, tiles, channels = x.shape
    rows = positions * tiles
    return pl.pallas_call(
        prepare_kernel,
        out_shape=(
            jax.ShapeDtypeStruct((rows, channels), jnp.bfloat16),
            jax.ShapeDtypeStruct((rows, channels), jnp.float32),
            jax.ShapeDtypeStruct((rows, LANES), jnp.float32),
            jax.ShapeDtypeStruct((tiles, channels), jnp.float32),
        ),
        in_specs=whole_vmem(5),
        out_specs=tuple(whole_vmem(4)),
        scratch_shapes=[
            pltpu.VMEM((positions, tiles, LANES), jnp.float32),
            pltpu.VMEM((positions, channels), jnp.float32),
        ],
        compiler_params=pltpu.CompilerParams(vmem_limit_bytes=VMEM_LIMIT),
        cost_estimate=pl.CostEstimate(flops=40_000_000, bytes_accessed=5_000_000, transcendentals=0),
    )(x, kernel, bias, gain, shift)


ROWS_STEP = 112


def hidden_kernel(normed_ref, w_ref, bias_ref, pooled_ref, slope_ref, hid):
    rows = normed_ref.shape[0]
    tiles, width = pooled_ref.shape
    hid[...] = lax.dot_general(
        normed_ref[...], w_ref[...], (((1,), (1,)), ((), ())), preferred_element_type=jnp.float32
    )
    bias = bias_ref[...].astype(jnp.float32)
    for c in range(width // LANES):
        lanes = slice(c * LANES, (c + 1) * LANES)
        part_bias = jnp.broadcast_to(bias[:, lanes], (tiles, LANES))

        def step(p, total):
            at = pl.ds(pl.multiple_of(p * tiles, tiles), tiles)
            h = hid[at, lanes] + part_bias
            cdf = 0.5 + 0.5 * lax.erf(h * (0.5 ** 0.5))
            pdf = jnp.exp(h * h * -0.5) * ((2.0 * math.pi) ** -0.5)
            active = (h * cdf).astype(jnp.bfloat16)
            slope_ref[at, lanes] = cdf + h * pdf
            return total + active.astype(jnp.float32)

        pooled_ref[:, lanes] = lax.fori_loop(
            0, rows // tiles, step, jnp.zeros((tiles, LANES), jnp.float32), unroll=7
        )


def hidden_layer(normed, w_in, in_bias, tiles):
    rows, channels = normed.shape
    ff = w_in.shape[0]
    width = 512
    return pl.pallas_call(
        hidden_kernel,
        grid=(ff // width,),
        out_shape=(
            jax.ShapeDtypeStruct((tiles, ff), jnp.float32),
            jax.ShapeDtypeStruct((rows, ff), jnp.float32),
        ),
        in_specs=[
            pl.BlockSpec((rows, channels), lambda f: (0, 0)),
            pl.BlockSpec((width, channels), lambda f: (f, 0)),
            pl.BlockSpec((1, width), lambda f: (0, f)),
        ],
        out_specs=(
            pl.BlockSpec((tiles, width), lambda f: (0, f)),
            pl.BlockSpec((rows, width), lambda f: (0, f)),
        ),
        scratch_shapes=[pltpu.VMEM((rows, width), jnp.float32)],
        compiler_params=pltpu.CompilerParams(vmem_limit_bytes=VMEM_LIMIT),
        cost_estimate=pl.CostEstimate(
            flops=2 * rows * ff * channels, bytes_accessed=20_000_000, transcendentals=rows * ff
        ),
    )(normed, w_in, in_bias)


def grad_hidden_kernel(slope_ref, ga_ref, normed_ref, gh_ref, gw_ref, gb_ref):
    rows = slope_ref.shape[0]
    tiles, width = ga_ref.shape
    for c in range(width // LANES):
        lanes = slice(c * LANES, (c + 1) * LANES)
        grad = ga_ref[:, lanes]

        def step(p, total):
            at = pl.ds(pl.multiple_of(p * tiles, tiles), tiles)
            wide = slope_ref[at, lanes] * grad
            gh_ref[at, lanes] = wide.astype(jnp.bfloat16)
            return total + wide

        total = lax.fori_loop(
            0, rows // tiles, step, jnp.zeros((tiles, LANES), jnp.float32), unroll=7
        )
        gb_ref[:, lanes] = jnp.sum(total, axis=0, keepdims=True)
    gw_ref[...] = lax.dot_general(
        gh_ref[...], normed_ref[...], (((0,), (0,)), ((), ())), preferred_element_type=jnp.float32
    )


def grad_hidden_layer(slope, grad_active, normed):
    rows, ff = slope.shape
    tiles = grad_active.shape[0]
    channels = normed.shape[1]
    width = 512
    return pl.pallas_call(
        grad_hidden_kernel,
        grid=(ff // width,),
        out_shape=(
            jax.ShapeDtypeStruct((rows, ff), jnp.bfloat16),
            jax.ShapeDtypeStruct((ff, channels), jnp.float32),
            jax.ShapeDtypeStruct((1, ff), jnp.float32),
        ),
        in_specs=[
            pl.BlockSpec((rows, width), lambda f: (0, f)),
            pl.BlockSpec((tiles, width), lambda f: (0, f)),
            pl.BlockSpec((rows, channels), lambda f: (0, 0)),
        ],
        out_specs=(
            pl.BlockSpec((rows, width), lambda f: (0, f)),
            pl.BlockSpec((width, channels), lambda f: (f, 0)),
            pl.BlockSpec((1, width), lambda f: (0, f)),
        ),
        compiler_params=pltpu.CompilerParams(vmem_limit_bytes=VMEM_LIMIT),
        cost_estimate=pl.CostEstimate(
            flops=2 * rows * ff * channels, bytes_accessed=25_000_000, transcendentals=0
        ),
    )(slope, grad_active, normed)


def prepare_back_kernel(gn_ref, hat_ref, rstd_ref, x_ref, gain_ref, out_ref, gc, xs):
    tiles, channels = x_ref.shape[1], x_ref.shape[2]
    gain = gain_ref[...].astype(jnp.float32)

    def norm(p, carry):
        total_gain, total_shift = carry
        rows = pl.ds(pl.multiple_of(p * tiles, tiles), tiles)
        grad = gn_ref[rows, :]
        hat = hat_ref[rows, :]
        rstd = rstd_ref[rows, 0:1]
        scaled = grad * gain
        first = jnp.mean(scaled, axis=-1, keepdims=True)
        second = jnp.mean(scaled * hat, axis=-1, keepdims=True)
        gc[p] = rstd * (scaled - first - hat * second)
        return (total_gain + grad * hat, total_shift + grad)

    zero = jnp.zeros((tiles, channels), jnp.float32)
    total_gain, total_shift = lax.fori_loop(0, POSITIONS, norm, (zero, zero))
    out_ref[pl.ds(POSITIONS + 1, 1), :] = jnp.sum(total_gain, axis=0, keepdims=True)
    out_ref[pl.ds(POSITIONS + 2, 1), :] = jnp.sum(total_shift, axis=0, keepdims=True)

    def block(c, carry):
        lanes = pl.ds(pl.multiple_of(c * LANES, LANES), LANES)
        total = jnp.zeros((tiles, LANES), jnp.float32)
        for p in range(POSITIONS):
            xs[p] = x_ref[p, :, lanes].astype(jnp.float32)
            total = total + gc[p, :, lanes]
        out_ref[pl.ds(POSITIONS, 1), lanes] = jnp.sum(total, axis=0, keepdims=True)
        for a in range(KERNEL):
            accs = [jnp.zeros((tiles, LANES), jnp.float32) for _ in range(KERNEL)]
            for i in range(SIDE):
                row = i + a - MARGIN
                if row < 0 or row >= SIDE:
                    continue
                grads = [gc[i * SIDE + j, :, lanes] for j in range(SIDE)]
                for col in range(SIDE):
                    value = xs[row * SIDE + col]
                    for j in range(SIDE):
                        b = col - j + MARGIN
                        if 0 <= b < KERNEL:
                            accs[b] = accs[b] + value * grads[j]
            for b in range(KERNEL):
                out_ref[pl.ds(a * KERNEL + b, 1), lanes] = jnp.sum(accs[b], axis=0, keepdims=True)
        return carry

    lax.fori_loop(0, channels // LANES, block, 0)


def prepare_back(grad_normed, hat, rstd, x, gain):
    positions, tiles, channels = x.shape
    return pl.pallas_call(
        prepare_back_kernel,
        out_shape=jax.ShapeDtypeStruct((positions + 3, channels), jnp.float32),
        in_specs=whole_vmem(5),
        out_specs=pl.BlockSpec(memory_space=pltpu.VMEM),
        scratch_shapes=[
            pltpu.VMEM((positions, tiles, channels), jnp.float32),
            pltpu.VMEM((positions, tiles, LANES), jnp.float32),
        ],
        compiler_params=pltpu.CompilerParams(vmem_limit_bytes=VMEM_LIMIT),
        cost_estimate=pl.CostEstimate(flops=40_000_000, bytes_accessed=8_000_000, transcendentals=0),
    )(grad_normed, hat, rstd, x, gain)


def swap(values, bit, devices):
    pairs = [(d, d ^ (1 << bit)) for d in range(devices)]
    return lax.ppermute(values, AXES, pairs)


def halve_scatter(partial_sum, order, narrow, devices, index):
    bits = devices.bit_length() - 1
    rows, columns = partial_sum.shape
    current = partial_sum.reshape((2,) * bits + (rows // devices, columns))
    left = list(range(bits - 1, -1, -1))
    for bit in order:
        axis = left.index(bit)
        left.pop(axis)
        mine = (index >> bit) & 1
        kept = lax.dynamic_index_in_dim(current, mine, axis, keepdims=False)
        sent = lax.dynamic_index_in_dim(current, 1 - mine, axis, keepdims=False)
        if bit in narrow:
            sent = sent.astype(jnp.bfloat16)
        shape = sent.shape
        flat = sent.reshape(-1, columns)
        current = kept + swap(flat, bit, devices).reshape(shape).astype(jnp.float32)
    return current


def per_device(
    tile_features, tile_slide, slide_order, targets, dw_kernel, dw_bias, norm_gain, norm_bias,
    w_in, in_bias, w_out, out_bias, layer_scale, final_gain, final_bias, head_weight, head_bias,
):
    highest = lax.Precision.HIGHEST
    f32 = jnp.float32
    bf16 = jnp.bfloat16
    tiles, channels = tile_features.shape[0], tile_features.shape[-1]
    ff = w_in.shape[0]
    n_enc, n_slide = lax.axis_size("enc"), lax.axis_size("slide")
    devices = n_enc * n_slide
    slides = slide_order.shape[1]
    owned = slides // n_slide
    genes = targets.shape[-1]
    enc_index, slide_index = lax.axis_index("enc"), lax.axis_index("slide")
    index = enc_index * n_slide + slide_index

    hot = (tile_slide == slide_order).astype(f32)
    tally = jnp.pad(jnp.sum(hot, axis=0)[None, :], ((0, 0), (0, -slides % genes)))
    early = lax.all_gather(
        jnp.concatenate([targets[0], tally.reshape(-1, genes)], axis=0), "slide"
    )
    all_targets = early[:, :owned].reshape(slides, genes)
    counts = jnp.sum(early[:, owned:].reshape(n_slide, -1), axis=0)[:slides]
    divisor = jnp.maximum(counts, 1.0)[:, None]

    x = jnp.transpose(tile_features, (1, 2, 0, 3)).reshape(POSITIONS, tiles, channels)
    normed, hat, rstd, feature_sum = prepare(
        x, dw_kernel, dw_bias[None, :], norm_gain[None, :], norm_bias[None, :]
    )
    pooled_active, slope = hidden_layer(normed, w_in, in_bias[None, :], tiles)
    high = lax.reduce_precision(pooled_active, 8, 7)
    both = jnp.concatenate([high, pooled_active - high], axis=0).astype(bf16)
    product = jnp.dot(both, w_out, preferred_element_type=f32)
    branch = (product[:tiles] + product[tiles:]) / POSITIONS + out_bias.astype(f32)
    scale = layer_scale.astype(f32)
    pooled = feature_sum / POSITIONS + scale * branch
    embedded, pull_norm = jax.vjp(
        layer_norm, pooled, final_gain.astype(f32), final_bias.astype(f32)
    )
    partial_sums = lax.dot_general(
        hot.astype(bf16), embedded.astype(bf16), (((0,), (0,)), ((), ())),
        preferred_element_type=f32,
    )
    slide_mean = jnp.sum(lax.all_gather(partial_sums, "slide"), axis=0) / divisor
    head_wide = head_weight.astype(f32)
    prediction = jnp.dot(
        slide_mean, head_wide, precision=highest, preferred_element_type=f32
    ) + head_bias.astype(f32)
    difference = prediction - all_targets
    losses = 0.5 * jnp.mean(difference * difference, axis=-1)
    slide_loss = lax.dynamic_slice_in_dim(losses, slide_index * owned, owned)
    grad_pred = difference / genes
    grad_mean = lax.dot_general(
        grad_pred, head_wide, (((1,), (1,)), ((), ())), precision=highest,
        preferred_element_type=f32,
    )
    slide_grad = (grad_mean / divisor).astype(bf16)
    grad_embed = jnp.dot(hot.astype(bf16), slide_grad, preferred_element_type=f32)
    grad_pooled, grad_fgain, grad_fbias = pull_norm(grad_embed)
    grad_scale = jnp.sum(grad_pooled * branch, axis=0)
    scaled = grad_pooled * scale
    grad_out_bias = jnp.sum(scaled, axis=0)
    grad_projected = (scaled / POSITIONS).astype(bf16)
    grad_active = lax.dot_general(
        grad_projected, w_out, (((1,), (1,)), ((), ())), preferred_element_type=f32
    )
    grad_hidden, partial_w_in, grad_inner = grad_hidden_layer(slope, grad_active, normed)

    bits = devices.bit_length() - 1
    inner = n_slide.bit_length() - 1
    xs = list(range(1, inner))
    rest = list(range(inner, bits))
    half = channels // 2
    narrow = (1, inner)
    first = halve_scatter(
        partial_w_in[:, :half], [0] + xs + rest, narrow, devices, index
    )
    second = halve_scatter(
        partial_w_in[:, half:], [0] + rest[:1] + xs + rest[1:], narrow, devices, index
    )
    grad_w_in = jnp.concatenate([first, second], axis=1)

    grad_normed = jnp.dot(grad_hidden, w_in, preferred_element_type=f32)
    small = prepare_back(grad_normed, hat, rstd, x, norm_gain[None, :])
    bundle = jnp.concatenate(
        [
            small, grad_out_bias[None], grad_scale[None], grad_fgain[None], grad_fbias[None],
            grad_inner.reshape(-1, channels),
        ],
        axis=0,
    )
    used = bundle.shape[0]
    bundle = jnp.pad(bundle, ((0, -used % 64), (0, 0)))
    lines = bundle.reshape(devices, -1)
    lines = lax.all_to_all(lines, AXES, split_axis=0, concat_axis=0, tiled=True)
    bundle = lax.all_gather(jnp.sum(lines, axis=0), AXES).reshape(-1, channels)

    head_parts = lax.all_gather(
        jnp.concatenate([slide_mean, grad_pred], axis=1), "enc"
    ).reshape(n_enc * slides, channels + genes)
    grad_head_w = lax.dot_general(
        head_parts[:, :channels], head_parts[:, channels:], (((0,), (0,)), ((), ())),
        precision=highest, preferred_element_type=f32,
    )
    grad_head_b = jnp.sum(head_parts[:, channels:], axis=0)

    mine = pooled_active.reshape(tiles, devices, ff // devices).transpose(1, 0, 2)
    mine = lax.all_to_all(mine, AXES, split_axis=0, concat_axis=0, tiled=True)
    mine = mine.reshape(devices * tiles, ff // devices)
    mine_high = lax.reduce_precision(mine, 8, 7)
    all_grad = lax.all_gather(grad_projected, AXES, tiled=True)

    def rows_product(left):
        return lax.dot_general(
            left.astype(bf16), all_grad, (((0,), (0,)), ((), ())), preferred_element_type=f32
        )

    grad_w_out = rows_product(mine_high) + rows_product(mine - mine_high)
    taps = POSITIONS
    return (
        grad_w_in,
        grad_w_out,
        bundle[:taps],
        bundle[taps : taps + 7],
        bundle[taps + 7 : used].reshape(-1),
        grad_head_w,
        grad_head_b,
        slide_loss[None, :],
    )


def solution(mesh):
    placed = (
        P(AXES, None, None, None),
        P(AXES, None),
        P("enc", None),
        P("enc", "slide", None),
    ) + (P(),) * 13
    return jax.shard_map(
        per_device,
        mesh=mesh,
        in_specs=placed,
        out_specs=(P(AXES, None), P(AXES, None), P(), P(), P(), P(), P(), P("enc", "slide")),
        check_vma=False,
    )
```

```python
import math
from functools import partial

import jax
import jax.numpy as jnp
from jax import lax
from jax.experimental import pallas as pl
from jax.experimental.pallas import tpu as pltpu
from jax.sharding import PartitionSpec as P

KERNEL = 7
SIDE = 7
MARGIN = KERNEL // 2
POSITIONS = SIDE * SIDE
LANES = 128
EPSILON = 1e-06
VMEM_LIMIT = 56 * 1024 * 1024
AXES = ("enc", "slide")


def layer_norm(values, gain, shift):
    center = values - jnp.mean(values, axis=-1, keepdims=True)
    spread = jnp.mean(center * center, axis=-1, keepdims=True)
    return center * lax.rsqrt(spread + EPSILON) * gain + shift


def whole_vmem(count):
    return [pl.BlockSpec(memory_space=pltpu.VMEM)] * count


def prepare_kernel(x_ref, k_ref, vec_ref, normed_ref, hat_ref, rstd_ref, fsum_ref, xs, ks):
    tiles, channels = x_ref.shape[1], x_ref.shape[2]
    ks[...] = k_ref[...].astype(jnp.float32)

    def block(c, carry):
        lanes = pl.ds(pl.multiple_of(c * LANES, LANES), LANES)
        total = jnp.zeros((tiles, LANES), jnp.float32)
        for p in range(POSITIONS):
            value = x_ref[p, :, lanes].astype(jnp.float32)
            xs[p] = value
            total = total + value
        fsum_ref[:, lanes] = total
        bias = jnp.broadcast_to(vec_ref[0:1, lanes], (tiles, LANES))
        for i in range(SIDE):
            accs = [bias for _ in range(SIDE)]
            for a in range(KERNEL):
                row = i + a - MARGIN
                if row < 0 or row >= SIDE:
                    continue
                weights = [ks[pl.ds(a * KERNEL + b, 1), lanes] for b in range(KERNEL)]
                for col in range(SIDE):
                    value = xs[row * SIDE + col]
                    for j in range(SIDE):
                        b = col - j + MARGIN
                        if 0 <= b < KERNEL:
                            accs[j] = accs[j] + value * weights[b]
            for j in range(SIDE):
                rows = pl.ds((i * SIDE + j) * tiles, tiles)
                hat_ref[rows, lanes] = accs[j]
        return carry

    lax.fori_loop(0, channels // LANES, block, 0)
    gain = vec_ref[1:2, :]
    shift = vec_ref[2:3, :]

    def norm(p, carry):
        rows = pl.ds(pl.multiple_of(p * tiles, tiles), tiles)
        conv = hat_ref[rows, :]
        center = conv - jnp.mean(conv, axis=-1, keepdims=True)
        spread = jnp.mean(center * center, axis=-1, keepdims=True)
        rstd = lax.rsqrt(spread + EPSILON)
        hat = center * rstd
        hat_ref[rows, :] = hat
        normed_ref[rows, :] = (hat * gain + shift).astype(jnp.bfloat16)
        rstd_ref[rows, :] = jnp.broadcast_to(rstd, (tiles, LANES))
        return carry

    lax.fori_loop(0, POSITIONS, norm, 0, unroll=7)


def prepare(x, kernel, vectors):
    positions, tiles, channels = x.shape
    rows = positions * tiles
    return pl.pallas_call(
        prepare_kernel,
        out_shape=(
            jax.ShapeDtypeStruct((rows, channels), jnp.bfloat16),
            jax.ShapeDtypeStruct((rows, channels), jnp.float32),
            jax.ShapeDtypeStruct((rows, LANES), jnp.float32),
            jax.ShapeDtypeStruct((tiles, channels), jnp.float32),
        ),
        in_specs=whole_vmem(3),
        out_specs=tuple(whole_vmem(4)),
        scratch_shapes=[
            pltpu.VMEM((positions, tiles, LANES), jnp.float32),
            pltpu.VMEM((positions, channels), jnp.float32),
        ],
        compiler_params=pltpu.CompilerParams(vmem_limit_bytes=VMEM_LIMIT),
        cost_estimate=pl.CostEstimate(flops=40_000_000, bytes_accessed=5_000_000, transcendentals=0),
    )(x, kernel, vectors)


def hidden_kernel(normed_ref, w_ref, bias_ref, pooled_ref, slope_ref, hid):
    rows = normed_ref.shape[0]
    tiles, width = pooled_ref.shape
    hid[...] = lax.dot_general(
        normed_ref[...], w_ref[...], (((1,), (1,)), ((), ())), preferred_element_type=jnp.float32
    )
    bias = bias_ref[...].astype(jnp.float32)
    for c in range(width // LANES):
        lanes = slice(c * LANES, (c + 1) * LANES)
        part_bias = jnp.broadcast_to(bias[:, lanes], (tiles, LANES))

        def step(p, total):
            at = pl.ds(pl.multiple_of(p * tiles, tiles), tiles)
            h = hid[at, lanes] + part_bias
            cdf = 0.5 + 0.5 * lax.erf(h * (0.5 ** 0.5))
            pdf = jnp.exp(h * h * -0.5) * ((2.0 * math.pi) ** -0.5)
            active = (h * cdf).astype(jnp.bfloat16)
            slope_ref[at, lanes] = cdf + h * pdf
            return total + active.astype(jnp.float32)

        pooled_ref[:, lanes] = lax.fori_loop(
            0, rows // tiles, step, jnp.zeros((tiles, LANES), jnp.float32), unroll=7
        )


def hidden_layer(normed, w_in, in_bias, tiles):
    rows, channels = normed.shape
    ff = w_in.shape[0]
    width = 512
    return pl.pallas_call(
        hidden_kernel,
        grid=(ff // width,),
        out_shape=(
            jax.ShapeDtypeStruct((tiles, ff), jnp.float32),
            jax.ShapeDtypeStruct((rows, ff), jnp.float32),
        ),
        in_specs=[
            pl.BlockSpec((rows, channels), lambda f: (0, 0)),
            pl.BlockSpec((width, channels), lambda f: (f, 0)),
            pl.BlockSpec((1, width), lambda f: (0, f)),
        ],
        out_specs=(
            pl.BlockSpec((tiles, width), lambda f: (0, f)),
            pl.BlockSpec((rows, width), lambda f: (0, f)),
        ),
        scratch_shapes=[pltpu.VMEM((rows, width), jnp.float32)],
        compiler_params=pltpu.CompilerParams(vmem_limit_bytes=VMEM_LIMIT),
        cost_estimate=pl.CostEstimate(
            flops=2 * rows * ff * channels, bytes_accessed=20_000_000, transcendentals=rows * ff
        ),
    )(normed, w_in, in_bias)


def grad_hidden_kernel(slope_ref, ga_ref, normed_ref, gh_ref, first_ref, second_ref, gb_ref):
    rows = slope_ref.shape[0]
    tiles, width = ga_ref.shape
    for c in range(width // LANES):
        lanes = slice(c * LANES, (c + 1) * LANES)
        grad = ga_ref[:, lanes]

        def step(p, total):
            at = pl.ds(pl.multiple_of(p * tiles, tiles), tiles)
            wide = slope_ref[at, lanes] * grad
            gh_ref[at, lanes] = wide.astype(jnp.bfloat16)
            return total + wide

        total = lax.fori_loop(
            0, rows // tiles, step, jnp.zeros((tiles, LANES), jnp.float32), unroll=7
        )
        gb_ref[:, lanes] = jnp.sum(total, axis=0, keepdims=True)
    whole = lax.dot_general(
        gh_ref[...], normed_ref[...], (((0,), (0,)), ((), ())), preferred_element_type=jnp.float32
    )
    half = first_ref.shape[1]
    first_ref[...] = whole[:, :half]
    second_ref[...] = whole[:, half:]


def grad_hidden_layer(slope, grad_active, normed):
    rows, ff = slope.shape
    tiles = grad_active.shape[0]
    channels = normed.shape[1]
    width = 512
    return pl.pallas_call(
        grad_hidden_kernel,
        grid=(ff // width,),
        out_shape=(
            jax.ShapeDtypeStruct((rows, ff), jnp.bfloat16),
            jax.ShapeDtypeStruct((ff, channels // 2), jnp.float32),
            jax.ShapeDtypeStruct((ff, channels // 2), jnp.float32),
            jax.ShapeDtypeStruct((1, ff), jnp.float32),
        ),
        in_specs=[
            pl.BlockSpec((rows, width), lambda f: (0, f)),
            pl.BlockSpec((tiles, width), lambda f: (0, f)),
            pl.BlockSpec((rows, channels), lambda f: (0, 0)),
        ],
        out_specs=(
            pl.BlockSpec((rows, width), lambda f: (0, f)),
            pl.BlockSpec((width, channels // 2), lambda f: (f, 0)),
            pl.BlockSpec((width, channels // 2), lambda f: (f, 0)),
            pl.BlockSpec((1, width), lambda f: (0, f)),
        ),
        compiler_params=pltpu.CompilerParams(vmem_limit_bytes=VMEM_LIMIT),
        cost_estimate=pl.CostEstimate(
            flops=2 * rows * ff * channels, bytes_accessed=25_000_000, transcendentals=0
        ),
    )(slope, grad_active, normed)


def prepare_back_kernel(gn_ref, hat_ref, rstd_ref, x_ref, vec_ref, out_ref, gc, xs):
    tiles, channels = x_ref.shape[1], x_ref.shape[2]
    gain = vec_ref[1:2, :]

    def norm(p, carry):
        total_gain, total_shift = carry
        rows = pl.ds(pl.multiple_of(p * tiles, tiles), tiles)
        grad = gn_ref[rows, :]
        hat = hat_ref[rows, :]
        rstd = rstd_ref[rows, 0:1]
        scaled = grad * gain
        first = jnp.mean(scaled, axis=-1, keepdims=True)
        second = jnp.mean(scaled * hat, axis=-1, keepdims=True)
        gc[p] = rstd * (scaled - first - hat * second)
        return (total_gain + grad * hat, total_shift + grad)

    zero = jnp.zeros((tiles, channels), jnp.float32)
    total_gain, total_shift = lax.fori_loop(0, POSITIONS, norm, (zero, zero))
    out_ref[pl.ds(POSITIONS + 1, 1), :] = jnp.sum(total_gain, axis=0, keepdims=True)
    out_ref[pl.ds(POSITIONS + 2, 1), :] = jnp.sum(total_shift, axis=0, keepdims=True)

    def block(c, carry):
        lanes = pl.ds(pl.multiple_of(c * LANES, LANES), LANES)
        total = jnp.zeros((tiles, LANES), jnp.float32)
        for p in range(POSITIONS):
            xs[p] = x_ref[p, :, lanes].astype(jnp.float32)
            total = total + gc[p, :, lanes]
        out_ref[pl.ds(POSITIONS, 1), lanes] = jnp.sum(total, axis=0, keepdims=True)
        for a in range(KERNEL):
            accs = [jnp.zeros((tiles, LANES), jnp.float32) for _ in range(KERNEL)]
            for i in range(SIDE):
                row = i + a - MARGIN
                if row < 0 or row >= SIDE:
                    continue
                grads = [gc[i * SIDE + j, :, lanes] for j in range(SIDE)]
                for col in range(SIDE):
                    value = xs[row * SIDE + col]
                    for j in range(SIDE):
                        b = col - j + MARGIN
                        if 0 <= b < KERNEL:
                            accs[b] = accs[b] + value * grads[j]
            for b in range(KERNEL):
                out_ref[pl.ds(a * KERNEL + b, 1), lanes] = jnp.sum(accs[b], axis=0, keepdims=True)
        return carry

    lax.fori_loop(0, channels // LANES, block, 0)


def prepare_back(grad_normed, hat, rstd, x, vectors):
    positions, tiles, channels = x.shape
    return pl.pallas_call(
        prepare_back_kernel,
        out_shape=jax.ShapeDtypeStruct((positions + 3, channels), jnp.float32),
        in_specs=whole_vmem(5),
        out_specs=pl.BlockSpec(memory_space=pltpu.VMEM),
        scratch_shapes=[
            pltpu.VMEM((positions, tiles, channels), jnp.float32),
            pltpu.VMEM((positions, tiles, LANES), jnp.float32),
        ],
        compiler_params=pltpu.CompilerParams(vmem_limit_bytes=VMEM_LIMIT),
        cost_estimate=pl.CostEstimate(flops=40_000_000, bytes_accessed=8_000_000, transcendentals=0),
    )(grad_normed, hat, rstd, x, vectors)


def swap(values, bit, devices):
    pairs = [(d, d ^ (1 << bit)) for d in range(devices)]
    return lax.ppermute(values, AXES, pairs)


def halve_scatter(partial_sum, order, narrow, devices, index):
    bits = devices.bit_length() - 1
    rows, columns = partial_sum.shape
    current = partial_sum.reshape((2,) * bits + (rows // devices, columns))
    left = list(range(bits - 1, -1, -1))
    for bit in order:
        axis = left.index(bit)
        left.pop(axis)
        mine = (index >> bit) & 1
        kept = lax.dynamic_index_in_dim(current, mine, axis, keepdims=False)
        sent = lax.dynamic_index_in_dim(current, 1 - mine, axis, keepdims=False)
        if bit in narrow:
            sent = sent.astype(jnp.bfloat16)
        shape = sent.shape
        flat = sent.reshape(-1, columns)
        current = kept + swap(flat, bit, devices).reshape(shape).astype(jnp.float32)
    return current


def exchange_kernel(
    devices, n_slide, sums_ref, pooled_ref, grad_ref, head_ref,
    total_ref, all_pooled_ref, all_grad_ref, all_head_ref, landed, send_sem, recv_sem,
):
    me = lax.axis_index("enc") * n_slide + lax.axis_index("slide")

    def place(device):
        return {"enc": device // n_slide, "slide": lax.rem(device, n_slide)}

    def each(body):
        def step(k, carry):
            body(k, lax.rem(me + k, devices), lax.rem(me + devices - k, devices))
            return carry

        lax.fori_loop(1, devices, step, 0)

    def copy(kind, k, source, target, device):
        return pltpu.make_async_remote_copy(
            src_ref=source, dst_ref=target, send_sem=send_sem.at[kind, k],
            recv_sem=recv_sem.at[kind, k], device_id=place(device),
            device_id_type=pl.DeviceIdType.MESH,
        )

    barrier = pltpu.get_barrier_semaphore()
    each(lambda k, to, source: pl.semaphore_signal(
        barrier, inc=1, device_id=place(to), device_id_type=pl.DeviceIdType.MESH))
    pl.semaphore_wait(barrier, devices - 1)

    def sums(k, to, slot):
        return copy(0, k, sums_ref.at[to], landed.at[slot], to)

    def others(k, to, slot):
        return (
            copy(1, k, pooled_ref.at[to], all_pooled_ref.at[slot], to),
            copy(2, k, grad_ref, all_grad_ref.at[slot], to),
            copy(3, k, head_ref, all_head_ref.at[slot], to),
        )

    def totals(k, to, slot):
        return copy(4, k, total_ref.at[me], total_ref.at[slot], to)

    each(lambda k, to, source: sums(k, to, me).start())
    landed[me] = sums_ref[me]
    all_pooled_ref[me] = pooled_ref[me]
    all_grad_ref[me] = grad_ref[...]
    all_head_ref[me] = head_ref[...]

    def start_others(k, to, source):
        for item in others(k, to, me):
            item.start()

    each(start_others)
    each(lambda k, to, source: sums(k, to, source).wait_recv())
    total_ref[me] = jnp.sum(landed[...], axis=0)
    each(lambda k, to, source: totals(k, to, me).start())

    def finish(k, to, source):
        sums(k, to, me).wait_send()
        for item in others(k, to, source):
            item.wait_recv()
        for item in others(k, to, me):
            item.wait_send()
        totals(k, to, source).wait_recv()
        totals(k, to, me).wait_send()

    each(finish)


def exchange(devices, n_slide, sums, pooled, grad, head):
    return pl.pallas_call(
        partial(exchange_kernel, devices, n_slide),
        out_shape=(
            jax.ShapeDtypeStruct(sums.shape, sums.dtype),
            jax.ShapeDtypeStruct(pooled.shape, pooled.dtype),
            jax.ShapeDtypeStruct((devices,) + grad.shape, grad.dtype),
            jax.ShapeDtypeStruct((devices,) + head.shape, head.dtype),
        ),
        in_specs=whole_vmem(4),
        out_specs=tuple(whole_vmem(4)),
        scratch_shapes=[
            pltpu.VMEM(sums.shape, sums.dtype),
            pltpu.SemaphoreType.DMA((5, devices)),
            pltpu.SemaphoreType.DMA((5, devices)),
        ],
        compiler_params=pltpu.CompilerParams(
            collective_id=0, has_side_effects=True, vmem_limit_bytes=VMEM_LIMIT
        ),
        cost_estimate=pl.CostEstimate(
            flops=1_000_000, bytes_accessed=40_000_000, transcendentals=0
        ),
    )(sums, pooled, grad, head)


def per_device(
    tile_features, tile_slide, slide_order, targets, dw_kernel, dw_bias, norm_gain, norm_bias,
    w_in, in_bias, w_out, out_bias, layer_scale, final_gain, final_bias, head_weight, head_bias,
):
    highest = lax.Precision.HIGHEST
    f32 = jnp.float32
    bf16 = jnp.bfloat16
    tiles, channels = tile_features.shape[0], tile_features.shape[-1]
    ff = w_in.shape[0]
    n_enc, n_slide = lax.axis_size("enc"), lax.axis_size("slide")
    devices = n_enc * n_slide
    slides = slide_order.shape[1]
    owned = slides // n_slide
    genes = targets.shape[-1]
    enc_index, slide_index = lax.axis_index("enc"), lax.axis_index("slide")
    index = enc_index * n_slide + slide_index

    hot = (tile_slide == slide_order).astype(f32)
    early = jnp.concatenate([targets.reshape(-1), jnp.sum(hot, axis=0)])
    early = jnp.pad(early, (0, -early.shape[0] % channels)).reshape(-1, channels)

    x = jnp.transpose(tile_features, (1, 2, 0, 3)).reshape(POSITIONS, tiles, channels)
    vectors = jnp.stack([dw_bias, norm_gain, norm_bias]).astype(f32)
    normed, hat, rstd, feature_sum = prepare(x, dw_kernel, vectors)
    pooled_active, slope = hidden_layer(normed, w_in, in_bias[None, :], tiles)
    high = lax.reduce_precision(pooled_active, 8, 7)
    both = jnp.concatenate([high, pooled_active - high], axis=0).astype(bf16)
    product = jnp.dot(both, w_out, preferred_element_type=f32)
    branch = (product[:tiles] + product[tiles:]) / POSITIONS + out_bias.astype(f32)
    scale = layer_scale.astype(f32)
    pooled = feature_sum / POSITIONS + scale * branch
    embedded, pull_norm = jax.vjp(
        layer_norm, pooled, final_gain.astype(f32), final_bias.astype(f32)
    )
    partial_sums = lax.dot_general(
        hot.astype(bf16), embedded.astype(bf16), (((0,), (0,)), ((), ())),
        preferred_element_type=f32,
    )
    group = lax.all_gather(jnp.concatenate([partial_sums, early], axis=0), "slide")
    early = group[:, slides:].reshape(n_slide, -1)
    all_targets = early[:, : owned * genes].reshape(slides, genes)
    counts = jnp.sum(early[:, owned * genes : owned * genes + slides], axis=0)
    divisor = jnp.maximum(counts, 1.0)[:, None]
    slide_mean = jnp.sum(group[:, :slides], axis=0) / divisor
    head_wide = head_weight.astype(f32)
    prediction = jnp.dot(
        slide_mean, head_wide, precision=highest, preferred_element_type=f32
    ) + head_bias.astype(f32)
    difference = prediction - all_targets
    losses = 0.5 * jnp.mean(difference * difference, axis=-1)
    slide_loss = lax.dynamic_slice_in_dim(losses, slide_index * owned, owned)
    grad_pred = difference / genes
    grad_mean = lax.dot_general(
        grad_pred, head_wide, (((1,), (1,)), ((), ())), precision=highest,
        preferred_element_type=f32,
    )
    slide_grad = (grad_mean / divisor).astype(bf16)
    grad_embed = jnp.dot(hot.astype(bf16), slide_grad, preferred_element_type=f32)
    grad_pooled, grad_fgain, grad_fbias = pull_norm(grad_embed)
    grad_scale = jnp.sum(grad_pooled * branch, axis=0)
    scaled = grad_pooled * scale
    grad_out_bias = jnp.sum(scaled, axis=0)
    grad_projected = (scaled / POSITIONS).astype(bf16)
    grad_active = lax.dot_general(
        grad_projected, w_out, (((1,), (1,)), ((), ())), preferred_element_type=f32
    )
    grad_hidden, first, second, grad_inner = grad_hidden_layer(slope, grad_active, normed)

    bits = devices.bit_length() - 1
    inner = n_slide.bit_length() - 1
    xs = list(range(1, inner))
    rest = list(range(inner, bits))
    narrow = (1, inner)
    first = halve_scatter(first, [0] + xs + rest, narrow, devices, index)
    second = halve_scatter(second, [0] + rest[:1] + xs + rest[1:], narrow, devices, index)
    grad_w_in = jnp.concatenate([first, second], axis=1)

    grad_normed = jnp.dot(grad_hidden, w_in, preferred_element_type=f32)
    small = prepare_back(grad_normed, hat, rstd, x, vectors)
    bundle = jnp.concatenate(
        [
            small, grad_out_bias[None], grad_scale[None], grad_fgain[None], grad_fbias[None],
            grad_inner.reshape(-1, channels),
        ],
        axis=0,
    )
    used = bundle.shape[0]
    bundle = jnp.pad(bundle, ((0, -used % devices), (0, 0))).reshape(devices, -1, channels)
    mine = pooled_active.reshape(tiles, devices, ff // devices).transpose(1, 0, 2)
    head_rows = lax.dynamic_slice_in_dim(
        jnp.concatenate([slide_mean, grad_pred], axis=1), slide_index * owned, owned
    )
    bundle, mine, all_grad, head_parts = exchange(
        devices, n_slide, bundle, mine, grad_projected, head_rows
    )
    bundle = bundle.reshape(-1, channels)
    head_parts = head_parts.reshape(-1, channels + genes)
    grad_head_w = lax.dot_general(
        head_parts[:, :channels], head_parts[:, channels:], (((0,), (0,)), ((), ())),
        precision=highest, preferred_element_type=f32,
    )
    grad_head_b = jnp.sum(head_parts[:, channels:], axis=0)
    mine = mine.reshape(devices * tiles, ff // devices)
    mine_high = lax.reduce_precision(mine, 8, 7)
    all_grad = all_grad.reshape(devices * tiles, channels)

    def rows_product(left):
        return lax.dot_general(
            left.astype(bf16), all_grad, (((0,), (0,)), ((), ())), preferred_element_type=f32
        )

    grad_w_out = rows_product(mine_high) + rows_product(mine - mine_high)
    taps = POSITIONS
    return (
        grad_w_in,
        grad_w_out,
        bundle[:taps],
        bundle[taps : taps + 7],
        bundle[taps + 7 : used].reshape(-1),
        grad_head_w,
        grad_head_b,
        slide_loss[None, :],
    )


def solution(mesh):
    placed = (
        P(AXES, None, None, None),
        P(AXES, None),
        P("enc", None),
        P("enc", "slide", None),
    ) + (P(),) * 13
    return jax.shard_map(
        per_device,
        mesh=mesh,
        in_specs=placed,
        out_specs=(P(AXES, None), P(AXES, None), P(), P(), P(), P(), P(), P("enc", "slide")),
        check_vma=False,
    )
```

```python
import math
from functools import partial

import jax
import jax.numpy as jnp
from jax import lax
from jax.experimental import pallas as pl
from jax.experimental.pallas import tpu as pltpu
from jax.sharding import PartitionSpec as P

KERNEL = 7
SIDE = 7
MARGIN = KERNEL // 2
POSITIONS = SIDE * SIDE
LANES = 128
EPSILON = 1e-06
VMEM_LIMIT = 56 * 1024 * 1024
AXES = ("enc", "slide")


def layer_norm(values, gain, shift):
    center = values - jnp.mean(values, axis=-1, keepdims=True)
    spread = jnp.mean(center * center, axis=-1, keepdims=True)
    return center * lax.rsqrt(spread + EPSILON) * gain + shift


def whole_vmem(count):
    return [pl.BlockSpec(memory_space=pltpu.VMEM)] * count


def prepare_kernel(x_ref, k_ref, vec_ref, normed_ref, hat_ref, rstd_ref, fsum_ref, xs, ks):
    tiles, channels = x_ref.shape[1], x_ref.shape[2]
    ks[...] = k_ref[...].astype(jnp.float32)

    def block(c, carry):
        lanes = pl.ds(pl.multiple_of(c * LANES, LANES), LANES)
        total = jnp.zeros((tiles, LANES), jnp.float32)
        for p in range(POSITIONS):
            value = x_ref[p, :, lanes].astype(jnp.float32)
            xs[p] = value
            total = total + value
        fsum_ref[:, lanes] = total
        bias = jnp.broadcast_to(vec_ref[0:1, lanes], (tiles, LANES))
        for i in range(SIDE):
            accs = [bias for _ in range(SIDE)]
            for a in range(KERNEL):
                row = i + a - MARGIN
                if row < 0 or row >= SIDE:
                    continue
                weights = [ks[pl.ds(a * KERNEL + b, 1), lanes] for b in range(KERNEL)]
                for col in range(SIDE):
                    value = xs[row * SIDE + col]
                    for j in range(SIDE):
                        b = col - j + MARGIN
                        if 0 <= b < KERNEL:
                            accs[j] = accs[j] + value * weights[b]
            for j in range(SIDE):
                rows = pl.ds((i * SIDE + j) * tiles, tiles)
                hat_ref[rows, lanes] = accs[j]
        return carry

    lax.fori_loop(0, channels // LANES, block, 0)
    gain = vec_ref[1:2, :]
    shift = vec_ref[2:3, :]

    def norm(p, carry):
        rows = pl.ds(pl.multiple_of(p * tiles, tiles), tiles)
        conv = hat_ref[rows, :]
        center = conv - jnp.mean(conv, axis=-1, keepdims=True)
        spread = jnp.mean(center * center, axis=-1, keepdims=True)
        rstd = lax.rsqrt(spread + EPSILON)
        hat = center * rstd
        hat_ref[rows, :] = hat
        normed_ref[rows, :] = (hat * gain + shift).astype(jnp.bfloat16)
        rstd_ref[rows, :] = jnp.broadcast_to(rstd, (tiles, LANES))
        return carry

    lax.fori_loop(0, POSITIONS, norm, 0, unroll=7)


def prepare(x, kernel, vectors):
    positions, tiles, channels = x.shape
    rows = positions * tiles
    return pl.pallas_call(
        prepare_kernel,
        out_shape=(
            jax.ShapeDtypeStruct((rows, channels), jnp.bfloat16),
            jax.ShapeDtypeStruct((rows, channels), jnp.float32),
            jax.ShapeDtypeStruct((rows, LANES), jnp.float32),
            jax.ShapeDtypeStruct((tiles, channels), jnp.float32),
        ),
        in_specs=whole_vmem(3),
        out_specs=tuple(whole_vmem(4)),
        scratch_shapes=[
            pltpu.VMEM((positions, tiles, LANES), jnp.float32),
            pltpu.VMEM((positions, channels), jnp.float32),
        ],
        compiler_params=pltpu.CompilerParams(vmem_limit_bytes=VMEM_LIMIT),
        cost_estimate=pl.CostEstimate(flops=40_000_000, bytes_accessed=5_000_000, transcendentals=0),
    )(x, kernel, vectors)


def hidden_kernel(normed_ref, w_ref, bias_ref, pooled_ref, slope_ref, hid):
    rows = normed_ref.shape[0]
    tiles, width = pooled_ref.shape
    hid[...] = lax.dot_general(
        normed_ref[...], w_ref[...], (((1,), (1,)), ((), ())), preferred_element_type=jnp.float32
    )
    bias = bias_ref[...].astype(jnp.float32)
    for c in range(width // LANES):
        lanes = slice(c * LANES, (c + 1) * LANES)
        part_bias = jnp.broadcast_to(bias[:, lanes], (tiles, LANES))

        def step(p, total):
            at = pl.ds(pl.multiple_of(p * tiles, tiles), tiles)
            h = hid[at, lanes] + part_bias
            cdf = 0.5 + 0.5 * lax.erf(h * (0.5 ** 0.5))
            pdf = jnp.exp(h * h * -0.5) * ((2.0 * math.pi) ** -0.5)
            active = (h * cdf).astype(jnp.bfloat16)
            slope_ref[at, lanes] = cdf + h * pdf
            return total + active.astype(jnp.float32)

        pooled_ref[:, lanes] = lax.fori_loop(
            0, rows // tiles, step, jnp.zeros((tiles, LANES), jnp.float32), unroll=7
        )


def hidden_layer(normed, w_in, in_bias, tiles):
    rows, channels = normed.shape
    ff = w_in.shape[0]
    width = 512
    return pl.pallas_call(
        hidden_kernel,
        grid=(ff // width,),
        out_shape=(
            jax.ShapeDtypeStruct((tiles, ff), jnp.float32),
            jax.ShapeDtypeStruct((rows, ff), jnp.float32),
        ),
        in_specs=[
            pl.BlockSpec((rows, channels), lambda f: (0, 0)),
            pl.BlockSpec((width, channels), lambda f: (f, 0)),
            pl.BlockSpec((1, width), lambda f: (0, f)),
        ],
        out_specs=(
            pl.BlockSpec((tiles, width), lambda f: (0, f)),
            pl.BlockSpec((rows, width), lambda f: (0, f)),
        ),
        scratch_shapes=[pltpu.VMEM((rows, width), jnp.float32)],
        compiler_params=pltpu.CompilerParams(vmem_limit_bytes=VMEM_LIMIT),
        cost_estimate=pl.CostEstimate(
            flops=2 * rows * ff * channels, bytes_accessed=20_000_000, transcendentals=rows * ff
        ),
    )(normed, w_in, in_bias)


def grad_hidden_kernel(slope_ref, ga_ref, normed_ref, gh_ref, first_ref, second_ref, gb_ref):
    rows = slope_ref.shape[0]
    tiles, width = ga_ref.shape
    for c in range(width // LANES):
        lanes = slice(c * LANES, (c + 1) * LANES)
        grad = ga_ref[:, lanes]

        def step(p, total):
            at = pl.ds(pl.multiple_of(p * tiles, tiles), tiles)
            wide = slope_ref[at, lanes] * grad
            gh_ref[at, lanes] = wide.astype(jnp.bfloat16)
            return total + wide

        total = lax.fori_loop(
            0, rows // tiles, step, jnp.zeros((tiles, LANES), jnp.float32), unroll=7
        )
        gb_ref[:, lanes] = jnp.sum(total, axis=0, keepdims=True)
    whole = lax.dot_general(
        gh_ref[...], normed_ref[...], (((0,), (0,)), ((), ())), preferred_element_type=jnp.float32
    )
    half = first_ref.shape[1]
    first_ref[...] = whole[:, :half]
    second_ref[...] = whole[:, half:]


def grad_hidden_layer(slope, grad_active, normed):
    rows, ff = slope.shape
    tiles = grad_active.shape[0]
    channels = normed.shape[1]
    width = 512
    return pl.pallas_call(
        grad_hidden_kernel,
        grid=(ff // width,),
        out_shape=(
            jax.ShapeDtypeStruct((rows, ff), jnp.bfloat16),
            jax.ShapeDtypeStruct((ff, channels // 2), jnp.float32),
            jax.ShapeDtypeStruct((ff, channels // 2), jnp.float32),
            jax.ShapeDtypeStruct((1, ff), jnp.float32),
        ),
        in_specs=[
            pl.BlockSpec((rows, width), lambda f: (0, f)),
            pl.BlockSpec((tiles, width), lambda f: (0, f)),
            pl.BlockSpec((rows, channels), lambda f: (0, 0)),
        ],
        out_specs=(
            pl.BlockSpec((rows, width), lambda f: (0, f)),
            pl.BlockSpec((width, channels // 2), lambda f: (f, 0)),
            pl.BlockSpec((width, channels // 2), lambda f: (f, 0)),
            pl.BlockSpec((1, width), lambda f: (0, f)),
        ),
        compiler_params=pltpu.CompilerParams(vmem_limit_bytes=VMEM_LIMIT),
        cost_estimate=pl.CostEstimate(
            flops=2 * rows * ff * channels, bytes_accessed=25_000_000, transcendentals=0
        ),
    )(slope, grad_active, normed)


def prepare_back_kernel(gn_ref, hat_ref, rstd_ref, x_ref, vec_ref, out_ref, gc, xs):
    tiles, channels = x_ref.shape[1], x_ref.shape[2]
    gain = vec_ref[1:2, :]

    def norm(p, carry):
        total_gain, total_shift = carry
        rows = pl.ds(pl.multiple_of(p * tiles, tiles), tiles)
        grad = gn_ref[rows, :]
        hat = hat_ref[rows, :]
        rstd = rstd_ref[rows, 0:1]
        scaled = grad * gain
        first = jnp.mean(scaled, axis=-1, keepdims=True)
        second = jnp.mean(scaled * hat, axis=-1, keepdims=True)
        gc[p] = rstd * (scaled - first - hat * second)
        return (total_gain + grad * hat, total_shift + grad)

    zero = jnp.zeros((tiles, channels), jnp.float32)
    total_gain, total_shift = lax.fori_loop(0, POSITIONS, norm, (zero, zero))
    out_ref[pl.ds(POSITIONS + 1, 1), :] = jnp.sum(total_gain, axis=0, keepdims=True)
    out_ref[pl.ds(POSITIONS + 2, 1), :] = jnp.sum(total_shift, axis=0, keepdims=True)

    def block(c, carry):
        lanes = pl.ds(pl.multiple_of(c * LANES, LANES), LANES)
        total = jnp.zeros((tiles, LANES), jnp.float32)
        for p in range(POSITIONS):
            xs[p] = x_ref[p, :, lanes].astype(jnp.float32)
            total = total + gc[p, :, lanes]
        out_ref[pl.ds(POSITIONS, 1), lanes] = jnp.sum(total, axis=0, keepdims=True)
        for a in range(KERNEL):
            accs = [jnp.zeros((tiles, LANES), jnp.float32) for _ in range(KERNEL)]
            for i in range(SIDE):
                row = i + a - MARGIN
                if row < 0 or row >= SIDE:
                    continue
                grads = [gc[i * SIDE + j, :, lanes] for j in range(SIDE)]
                for col in range(SIDE):
                    value = xs[row * SIDE + col]
                    for j in range(SIDE):
                        b = col - j + MARGIN
                        if 0 <= b < KERNEL:
                            accs[b] = accs[b] + value * grads[j]
            for b in range(KERNEL):
                out_ref[pl.ds(a * KERNEL + b, 1), lanes] = jnp.sum(accs[b], axis=0, keepdims=True)
        return carry

    lax.fori_loop(0, channels // LANES, block, 0)


def prepare_back(grad_normed, hat, rstd, x, vectors):
    positions, tiles, channels = x.shape
    return pl.pallas_call(
        prepare_back_kernel,
        out_shape=jax.ShapeDtypeStruct((positions + 3, channels), jnp.float32),
        in_specs=whole_vmem(5),
        out_specs=pl.BlockSpec(memory_space=pltpu.VMEM),
        scratch_shapes=[
            pltpu.VMEM((positions, tiles, channels), jnp.float32),
            pltpu.VMEM((positions, tiles, LANES), jnp.float32),
        ],
        compiler_params=pltpu.CompilerParams(vmem_limit_bytes=VMEM_LIMIT),
        cost_estimate=pl.CostEstimate(flops=10_000_000_000, bytes_accessed=40_000_000, transcendentals=0),
    )(grad_normed, hat, rstd, x, vectors)


def swap(values, bit, devices):
    pairs = [(d, d ^ (1 << bit)) for d in range(devices)]
    return lax.ppermute(values, AXES, pairs)


def halve_start(current, left, bit, narrow, devices, index):
    columns = current.shape[-1]
    axis = left.index(bit)
    mine = (index >> bit) & 1
    kept = lax.dynamic_index_in_dim(current, mine, axis, keepdims=False)
    sent = lax.dynamic_index_in_dim(current, 1 - mine, axis, keepdims=False)
    if bit in narrow:
        sent = sent.astype(jnp.bfloat16)
    arrived = swap(sent.reshape(-1, columns), bit, devices).reshape(sent.shape)
    return kept + arrived.astype(jnp.float32), left[:axis] + left[axis + 1 :]


def exchange_kernel(
    devices, n_slide, sums_ref, pooled_ref, grad_ref, head_ref,
    total_ref, all_pooled_ref, all_grad_ref, all_head_ref, landed, send_sem, recv_sem,
):
    n_enc = devices // n_slide
    my_enc, my_slide = lax.axis_index("enc"), lax.axis_index("slide")
    me = my_enc * n_slide + my_slide

    def slot_of(device):
        return lax.rem(device, n_slide) * n_enc + device // n_slide

    def place(device):
        return {"enc": device // n_slide, "slide": lax.rem(device, n_slide)}

    def each(body):
        def step(k, carry):
            body(k, lax.rem(me + k, devices), lax.rem(me + devices - k, devices))
            return carry

        lax.fori_loop(1, devices, step, 0)

    def copy(kind, k, source, target, device):
        return pltpu.make_async_remote_copy(
            src_ref=source, dst_ref=target, send_sem=send_sem.at[kind, k],
            recv_sem=recv_sem.at[kind, k], device_id=place(device),
            device_id_type=pl.DeviceIdType.MESH,
        )

    barrier = pltpu.get_barrier_semaphore()
    each(lambda k, to, source: pl.semaphore_signal(
        barrier, inc=1, device_id=place(to), device_id_type=pl.DeviceIdType.MESH))
    pl.semaphore_wait(barrier, devices - 1)

    def sums(k, to, slot):
        return copy(0, k, sums_ref.at[to], landed.at[slot], to)

    def pooled(k, to, slot):
        return copy(1, k, pooled_ref.at[to], all_pooled_ref.at[slot], to)

    def spread(k, to, slot):
        device = to * n_slide + my_slide
        return (
            copy(2, k, grad_ref, all_grad_ref.at[my_slide, slot], device),
            copy(3, k, head_ref, all_head_ref.at[my_slide, slot], device),
        )

    def each_enc(body):
        def step(k, carry):
            body(k, lax.rem(my_enc + k, n_enc), lax.rem(my_enc + n_enc - k, n_enc))
            return carry

        lax.fori_loop(1, n_enc, step, 0)

    def flip(value, bit):
        return value + (1 << bit) * (1 - 2 * lax.rem(value // (1 << bit), 2))

    def passed(bit, held, first, receive):
        peer = flip(my_slide, bit)
        items = []
        for q, mask in enumerate(held):
            slot = peer if receive else my_slide
            for m in mask:
                slot = flip(slot, m)
            for kind, ref in ((2, all_grad_ref), (3, all_head_ref)):
                items.append(copy(
                    kind, n_enc + first + q, ref.at[slot], ref.at[slot],
                    my_enc * n_slide + peer))
        return items

    def totals(k, to, slot):
        return copy(4, k, total_ref.at[me], total_ref.at[slot], to)

    each(lambda k, to, source: sums(k, to, me).start())
    landed[me] = sums_ref[me]
    all_pooled_ref[slot_of(me)] = pooled_ref[me]
    all_grad_ref[my_slide, my_enc] = grad_ref[...]
    all_head_ref[my_slide, my_enc] = head_ref[...]

    def start_spread(k, to, source):
        for item in spread(k, to, my_enc):
            item.start()

    def wait_spread(k, to, source):
        for item in spread(k, to, source):
            item.wait_recv()

    def sent_spread(k, to, source):
        for item in spread(k, to, my_enc):
            item.wait_send()

    each_enc(start_spread)
    each(lambda k, to, source: pooled(k, to, slot_of(me)).start())
    each(lambda k, to, source: sums(k, to, source).wait_recv())
    total_ref[me] = jnp.sum(landed[...], axis=0)
    each(lambda k, to, source: totals(k, to, me).start())
    each_enc(wait_spread)
    held, first = [()], 0
    sent = []
    for bit in range(n_slide.bit_length() - 2, -1, -1):
        outgoing = passed(bit, held, first, False)
        for item in outgoing:
            item.start()
        sent += outgoing
        for item in passed(bit, held, first, True):
            item.wait_recv()
        first += len(held)
        held = held + [mask + (bit,) for mask in held]
    for item in sent:
        item.wait_send()
    each_enc(sent_spread)

    def finish(k, to, source):
        sums(k, to, me).wait_send()
        pooled(k, to, slot_of(source)).wait_recv()
        pooled(k, to, slot_of(me)).wait_send()
        totals(k, to, source).wait_recv()
        totals(k, to, me).wait_send()

    each(finish)


def exchange(devices, n_slide, sums, pooled, grad, head):
    return pl.pallas_call(
        partial(exchange_kernel, devices, n_slide),
        out_shape=(
            jax.ShapeDtypeStruct(sums.shape, sums.dtype),
            jax.ShapeDtypeStruct(pooled.shape, pooled.dtype),
            jax.ShapeDtypeStruct((n_slide, devices // n_slide) + grad.shape, grad.dtype),
            jax.ShapeDtypeStruct((n_slide, devices // n_slide) + head.shape, head.dtype),
        ),
        in_specs=whole_vmem(4),
        out_specs=tuple(whole_vmem(4)),
        scratch_shapes=[
            pltpu.VMEM(sums.shape, sums.dtype),
            pltpu.SemaphoreType.DMA((5, devices)),
            pltpu.SemaphoreType.DMA((5, devices)),
        ],
        compiler_params=pltpu.CompilerParams(
            collective_id=0, has_side_effects=True, vmem_limit_bytes=VMEM_LIMIT
        ),
        cost_estimate=pl.CostEstimate(
            flops=1_000_000, bytes_accessed=40_000_000, transcendentals=0
        ),
    )(sums, pooled, grad, head)


def per_device(
    tile_features, tile_slide, slide_order, targets, dw_kernel, dw_bias, norm_gain, norm_bias,
    w_in, in_bias, w_out, out_bias, layer_scale, final_gain, final_bias, head_weight, head_bias,
):
    highest = lax.Precision.HIGHEST
    f32 = jnp.float32
    bf16 = jnp.bfloat16
    tiles, channels = tile_features.shape[0], tile_features.shape[-1]
    ff = w_in.shape[0]
    n_enc, n_slide = lax.axis_size("enc"), lax.axis_size("slide")
    devices = n_enc * n_slide
    slides = slide_order.shape[1]
    owned = slides // n_slide
    genes = targets.shape[-1]
    enc_index, slide_index = lax.axis_index("enc"), lax.axis_index("slide")
    index = enc_index * n_slide + slide_index

    hot = (tile_slide == slide_order).astype(f32)
    early = jnp.concatenate([targets.reshape(-1), jnp.sum(hot, axis=0)])
    early = jnp.pad(early, (0, -early.shape[0] % channels)).reshape(-1, channels)

    x = jnp.transpose(tile_features, (1, 2, 0, 3)).reshape(POSITIONS, tiles, channels)
    vectors = jnp.stack([dw_bias, norm_gain, norm_bias]).astype(f32)
    normed, hat, rstd, feature_sum = prepare(x, dw_kernel, vectors)
    pooled_active, slope = hidden_layer(normed, w_in, in_bias[None, :], tiles)
    high = lax.reduce_precision(pooled_active, 8, 7)
    both = jnp.concatenate([high, pooled_active - high], axis=0).astype(bf16)
    product = jnp.dot(both, w_out, preferred_element_type=f32)
    branch = (product[:tiles] + product[tiles:]) / POSITIONS + out_bias.astype(f32)
    scale = layer_scale.astype(f32)
    pooled = feature_sum / POSITIONS + scale * branch
    embedded, pull_norm = jax.vjp(
        layer_norm, pooled, final_gain.astype(f32), final_bias.astype(f32)
    )
    partial_sums = lax.dot_general(
        hot.astype(bf16), embedded.astype(bf16), (((0,), (0,)), ((), ())),
        preferred_element_type=f32,
    )
    group = lax.all_gather(jnp.concatenate([partial_sums, early], axis=0), "slide")
    early = group[:, slides:].reshape(n_slide, -1)
    all_targets = early[:, : owned * genes].reshape(slides, genes)
    counts = jnp.sum(early[:, owned * genes : owned * genes + slides], axis=0)
    divisor = jnp.maximum(counts, 1.0)[:, None]
    slide_mean = jnp.sum(group[:, :slides], axis=0) / divisor
    head_wide = head_weight.astype(f32)
    prediction = jnp.dot(
        slide_mean, head_wide, precision=highest, preferred_element_type=f32
    ) + head_bias.astype(f32)
    difference = prediction - all_targets
    losses = 0.5 * jnp.mean(difference * difference, axis=-1)
    slide_loss = lax.dynamic_slice_in_dim(losses, slide_index * owned, owned)
    grad_pred = difference / genes
    grad_mean = lax.dot_general(
        grad_pred, head_wide, (((1,), (1,)), ((), ())), precision=highest,
        preferred_element_type=f32,
    )
    slide_grad = (grad_mean / divisor).astype(bf16)
    grad_embed = jnp.dot(hot.astype(bf16), slide_grad, preferred_element_type=f32)
    grad_pooled, grad_fgain, grad_fbias = pull_norm(grad_embed)
    grad_scale = jnp.sum(grad_pooled * branch, axis=0)
    scaled = grad_pooled * scale
    grad_out_bias = jnp.sum(scaled, axis=0)
    grad_projected = (scaled / POSITIONS).astype(bf16)
    grad_active = lax.dot_general(
        grad_projected, w_out, (((1,), (1,)), ((), ())), preferred_element_type=f32
    )
    grad_hidden, first, second, grad_inner = grad_hidden_layer(slope, grad_active, normed)

    bits = devices.bit_length() - 1
    inner = n_slide.bit_length() - 1
    xs = list(range(1, inner))
    rest = list(range(inner, bits))
    narrow = (1, inner)
    orders = ([0] + xs + rest, [0] + rest[:1] + xs + rest[1:])
    current = [
        part.reshape((2,) * bits + (ff // devices, channels // 2)) for part in (first, second)
    ]
    left = [list(range(bits - 1, -1, -1))] * 2

    def stage(number):
        for part in range(2):
            current[part], left[part] = halve_start(
                current[part], left[part], orders[part][number], narrow, devices, index
            )

    stage(0)
    grad_normed = jnp.dot(grad_hidden, w_in, preferred_element_type=f32)
    grad_normed, current[0], current[1] = lax.optimization_barrier(
        (grad_normed, current[0], current[1])
    )
    stage(1)
    small = prepare_back(grad_normed, hat, rstd, x, vectors)
    small, current[0], current[1] = lax.optimization_barrier((small, current[0], current[1]))
    stage(2)
    bundle = jnp.concatenate(
        [
            small, grad_out_bias[None], grad_scale[None], grad_fgain[None], grad_fbias[None],
            grad_inner.reshape(-1, channels),
        ],
        axis=0,
    )
    used = bundle.shape[0]
    bundle = jnp.pad(bundle, ((0, -used % devices), (0, 0))).reshape(devices, -1, channels)
    mine = pooled_active.reshape(tiles, devices, ff // devices).transpose(1, 0, 2)
    head_rows = lax.dynamic_slice_in_dim(
        jnp.concatenate([slide_mean, grad_pred], axis=1), slide_index * owned, owned
    )
    bundle, mine, all_grad, head_parts = exchange(
        devices, n_slide, bundle, mine, grad_projected, head_rows
    )
    bundle, current[0], current[1] = lax.optimization_barrier((bundle, current[0], current[1]))
    for number in range(3, bits):
        stage(number)
    grad_w_in = jnp.concatenate(current, axis=1)
    bundle = bundle.reshape(-1, channels)
    head_parts = head_parts.reshape(-1, channels + genes)
    grad_head_w = lax.dot_general(
        head_parts[:, :channels], head_parts[:, channels:], (((0,), (0,)), ((), ())),
        precision=highest, preferred_element_type=f32,
    )
    grad_head_b = jnp.sum(head_parts[:, channels:], axis=0)
    mine = mine.reshape(devices * tiles, ff // devices)
    mine_high = lax.reduce_precision(mine, 8, 7)
    all_grad = all_grad.reshape(devices * tiles, channels)

    def rows_product(left):
        return lax.dot_general(
            left.astype(bf16), all_grad, (((0,), (0,)), ((), ())), preferred_element_type=f32
        )

    grad_w_out = rows_product(mine_high) + rows_product(mine - mine_high)
    taps = POSITIONS
    return (
        grad_w_in,
        grad_w_out,
        bundle[:taps],
        bundle[taps : taps + 7],
        bundle[taps + 7 : used].reshape(-1),
        grad_head_w,
        grad_head_b,
        slide_loss[None, :],
    )


def solution(mesh):
    placed = (
        P(AXES, None, None, None),
        P(AXES, None),
        P("enc", None),
        P("enc", "slide", None),
    ) + (P(),) * 13
    return jax.shard_map(
        per_device,
        mesh=mesh,
        in_specs=placed,
        out_specs=(P(AXES, None), P(AXES, None), P(), P(), P(), P(), P(), P("enc", "slide")),
        check_vma=False,
    )
```

```python
import math
from functools import partial

import jax
import jax.numpy as jnp
from jax import lax
from jax.experimental import pallas as pl
from jax.experimental.pallas import tpu as pltpu
from jax.sharding import PartitionSpec as P

KERNEL = 7
SIDE = 7
MARGIN = KERNEL // 2
POSITIONS = SIDE * SIDE
LANES = 128
EPSILON = 1e-06
VMEM_LIMIT = 56 * 1024 * 1024
AXES = ("enc", "slide")


def layer_norm(values, gain, shift):
    center = values - jnp.mean(values, axis=-1, keepdims=True)
    spread = jnp.mean(center * center, axis=-1, keepdims=True)
    return center * lax.rsqrt(spread + EPSILON) * gain + shift


def whole_vmem(count):
    return [pl.BlockSpec(memory_space=pltpu.VMEM)] * count


def prepare_kernel(x_ref, k_ref, vec_ref, normed_ref, hat_ref, rstd_ref, fsum_ref, xs, ks):
    tiles, channels = x_ref.shape[1], x_ref.shape[2]
    ks[...] = k_ref[...].astype(jnp.float32)

    def block(c, carry):
        lanes = pl.ds(pl.multiple_of(c * LANES, LANES), LANES)
        total = jnp.zeros((tiles, LANES), jnp.float32)
        for p in range(POSITIONS):
            value = x_ref[p, :, lanes].astype(jnp.float32)
            xs[p] = value
            total = total + value
        fsum_ref[:, lanes] = total
        bias = jnp.broadcast_to(vec_ref[0:1, lanes], (tiles, LANES))
        for i in range(SIDE):
            accs = [bias for _ in range(SIDE)]
            for a in range(KERNEL):
                row = i + a - MARGIN
                if row < 0 or row >= SIDE:
                    continue
                weights = [ks[pl.ds(a * KERNEL + b, 1), lanes] for b in range(KERNEL)]
                for col in range(SIDE):
                    value = xs[row * SIDE + col]
                    for j in range(SIDE):
                        b = col - j + MARGIN
                        if 0 <= b < KERNEL:
                            accs[j] = accs[j] + value * weights[b]
            for j in range(SIDE):
                rows = pl.ds((i * SIDE + j) * tiles, tiles)
                hat_ref[rows, lanes] = accs[j]
        return carry

    lax.fori_loop(0, channels // LANES, block, 0)
    gain = vec_ref[1:2, :]
    shift = vec_ref[2:3, :]

    def norm(p, carry):
        rows = pl.ds(pl.multiple_of(p * tiles, tiles), tiles)
        conv = hat_ref[rows, :]
        center = conv - jnp.mean(conv, axis=-1, keepdims=True)
        spread = jnp.mean(center * center, axis=-1, keepdims=True)
        rstd = lax.rsqrt(spread + EPSILON)
        hat = center * rstd
        hat_ref[rows, :] = hat
        normed_ref[rows, :] = (hat * gain + shift).astype(jnp.bfloat16)
        rstd_ref[rows, :] = jnp.broadcast_to(rstd, (tiles, LANES))
        return carry

    lax.fori_loop(0, POSITIONS, norm, 0, unroll=7)


def prepare(x, kernel, vectors):
    positions, tiles, channels = x.shape
    rows = positions * tiles
    return pl.pallas_call(
        prepare_kernel,
        out_shape=(
            jax.ShapeDtypeStruct((rows, channels), jnp.bfloat16),
            jax.ShapeDtypeStruct((rows, channels), jnp.float32),
            jax.ShapeDtypeStruct((rows, LANES), jnp.float32),
            jax.ShapeDtypeStruct((tiles, channels), jnp.float32),
        ),
        in_specs=whole_vmem(3),
        out_specs=tuple(whole_vmem(4)),
        scratch_shapes=[
            pltpu.VMEM((positions, tiles, LANES), jnp.float32),
            pltpu.VMEM((positions, channels), jnp.float32),
        ],
        compiler_params=pltpu.CompilerParams(vmem_limit_bytes=VMEM_LIMIT),
        cost_estimate=pl.CostEstimate(flops=40_000_000, bytes_accessed=5_000_000, transcendentals=0),
    )(x, kernel, vectors)


def hidden_kernel(normed_ref, w_ref, bias_ref, pooled_ref, slope_ref, hid):
    rows = normed_ref.shape[0]
    tiles, width = pooled_ref.shape
    hid[...] = lax.dot_general(
        normed_ref[...], w_ref[...], (((1,), (1,)), ((), ())), preferred_element_type=jnp.float32
    )
    bias = bias_ref[...].astype(jnp.float32)
    for c in range(width // LANES):
        lanes = slice(c * LANES, (c + 1) * LANES)
        part_bias = jnp.broadcast_to(bias[:, lanes], (tiles, LANES))

        def step(p, total):
            at = pl.ds(pl.multiple_of(p * tiles, tiles), tiles)
            h = hid[at, lanes] + part_bias
            cdf = 0.5 + 0.5 * lax.erf(h * (0.5 ** 0.5))
            pdf = jnp.exp(h * h * -0.5) * ((2.0 * math.pi) ** -0.5)
            active = (h * cdf).astype(jnp.bfloat16)
            slope_ref[at, lanes] = cdf + h * pdf
            return total + active.astype(jnp.float32)

        pooled_ref[:, lanes] = lax.fori_loop(
            0, rows // tiles, step, jnp.zeros((tiles, LANES), jnp.float32), unroll=7
        )


def hidden_layer(normed, w_in, in_bias, tiles):
    rows, channels = normed.shape
    ff = w_in.shape[0]
    width = 512
    return pl.pallas_call(
        hidden_kernel,
        grid=(ff // width,),
        out_shape=(
            jax.ShapeDtypeStruct((tiles, ff), jnp.float32),
            jax.ShapeDtypeStruct((rows, ff), jnp.float32),
        ),
        in_specs=[
            pl.BlockSpec((rows, channels), lambda f: (0, 0)),
            pl.BlockSpec((width, channels), lambda f: (f, 0)),
            pl.BlockSpec((1, width), lambda f: (0, f)),
        ],
        out_specs=(
            pl.BlockSpec((tiles, width), lambda f: (0, f)),
            pl.BlockSpec((rows, width), lambda f: (0, f)),
        ),
        scratch_shapes=[pltpu.VMEM((rows, width), jnp.float32)],
        compiler_params=pltpu.CompilerParams(vmem_limit_bytes=VMEM_LIMIT),
        cost_estimate=pl.CostEstimate(
            flops=2 * rows * ff * channels, bytes_accessed=20_000_000, transcendentals=rows * ff
        ),
    )(normed, w_in, in_bias)


def grad_hidden_kernel(slope_ref, ga_ref, normed_ref, gh_ref, first_ref, second_ref, gb_ref):
    rows = slope_ref.shape[0]
    tiles, width = ga_ref.shape
    for c in range(width // LANES):
        lanes = slice(c * LANES, (c + 1) * LANES)
        grad = ga_ref[:, lanes]

        def step(p, total):
            at = pl.ds(pl.multiple_of(p * tiles, tiles), tiles)
            wide = slope_ref[at, lanes] * grad
            gh_ref[at, lanes] = wide.astype(jnp.bfloat16)
            return total + wide

        total = lax.fori_loop(
            0, rows // tiles, step, jnp.zeros((tiles, LANES), jnp.float32), unroll=7
        )
        gb_ref[:, lanes] = jnp.sum(total, axis=0, keepdims=True)
    whole = lax.dot_general(
        gh_ref[...], normed_ref[...], (((0,), (0,)), ((), ())), preferred_element_type=jnp.float32
    )
    half = first_ref.shape[1]
    first_ref[...] = whole[:, :half]
    second_ref[...] = whole[:, half:]


def grad_hidden_layer(slope, grad_active, normed):
    rows, ff = slope.shape
    tiles = grad_active.shape[0]
    channels = normed.shape[1]
    width = 512
    return pl.pallas_call(
        grad_hidden_kernel,
        grid=(ff // width,),
        out_shape=(
            jax.ShapeDtypeStruct((rows, ff), jnp.bfloat16),
            jax.ShapeDtypeStruct((ff, channels // 2), jnp.float32),
            jax.ShapeDtypeStruct((ff, channels // 2), jnp.float32),
            jax.ShapeDtypeStruct((1, ff), jnp.float32),
        ),
        in_specs=[
            pl.BlockSpec((rows, width), lambda f: (0, f)),
            pl.BlockSpec((tiles, width), lambda f: (0, f)),
            pl.BlockSpec((rows, channels), lambda f: (0, 0)),
        ],
        out_specs=(
            pl.BlockSpec((rows, width), lambda f: (0, f)),
            pl.BlockSpec((width, channels // 2), lambda f: (f, 0)),
            pl.BlockSpec((width, channels // 2), lambda f: (f, 0)),
            pl.BlockSpec((1, width), lambda f: (0, f)),
        ),
        compiler_params=pltpu.CompilerParams(vmem_limit_bytes=VMEM_LIMIT),
        cost_estimate=pl.CostEstimate(
            flops=2 * rows * ff * channels, bytes_accessed=25_000_000, transcendentals=0
        ),
    )(slope, grad_active, normed)


def prepare_back_kernel(gn_ref, hat_ref, rstd_ref, x_ref, vec_ref, out_ref, gc, xs):
    tiles, channels = x_ref.shape[1], x_ref.shape[2]
    gain = vec_ref[1:2, :]

    def norm(p, carry):
        total_gain, total_shift = carry
        rows = pl.ds(pl.multiple_of(p * tiles, tiles), tiles)
        grad = gn_ref[rows, :]
        hat = hat_ref[rows, :]
        rstd = rstd_ref[rows, 0:1]
        scaled = grad * gain
        first = jnp.mean(scaled, axis=-1, keepdims=True)
        second = jnp.mean(scaled * hat, axis=-1, keepdims=True)
        gc[p] = rstd * (scaled - first - hat * second)
        return (total_gain + grad * hat, total_shift + grad)

    zero = jnp.zeros((tiles, channels), jnp.float32)
    total_gain, total_shift = lax.fori_loop(0, POSITIONS, norm, (zero, zero))
    out_ref[pl.ds(POSITIONS + 1, 1), :] = jnp.sum(total_gain, axis=0, keepdims=True)
    out_ref[pl.ds(POSITIONS + 2, 1), :] = jnp.sum(total_shift, axis=0, keepdims=True)

    def block(c, carry):
        lanes = pl.ds(pl.multiple_of(c * LANES, LANES), LANES)
        total = jnp.zeros((tiles, LANES), jnp.float32)
        for p in range(POSITIONS):
            xs[p] = x_ref[p, :, lanes].astype(jnp.float32)
            total = total + gc[p, :, lanes]
        out_ref[pl.ds(POSITIONS, 1), lanes] = jnp.sum(total, axis=0, keepdims=True)
        for a in range(KERNEL):
            accs = [jnp.zeros((tiles, LANES), jnp.float32) for _ in range(KERNEL)]
            for i in range(SIDE):
                row = i + a - MARGIN
                if row < 0 or row >= SIDE:
                    continue
                grads = [gc[i * SIDE + j, :, lanes] for j in range(SIDE)]
                for col in range(SIDE):
                    value = xs[row * SIDE + col]
                    for j in range(SIDE):
                        b = col - j + MARGIN
                        if 0 <= b < KERNEL:
                            accs[b] = accs[b] + value * grads[j]
            for b in range(KERNEL):
                out_ref[pl.ds(a * KERNEL + b, 1), lanes] = jnp.sum(accs[b], axis=0, keepdims=True)
        return carry

    lax.fori_loop(0, channels // LANES, block, 0)


def prepare_back(grad_normed, hat, rstd, x, vectors):
    positions, tiles, channels = x.shape
    return pl.pallas_call(
        prepare_back_kernel,
        out_shape=jax.ShapeDtypeStruct((positions + 3, channels), jnp.float32),
        in_specs=whole_vmem(5),
        out_specs=pl.BlockSpec(memory_space=pltpu.VMEM),
        scratch_shapes=[
            pltpu.VMEM((positions, tiles, channels), jnp.float32),
            pltpu.VMEM((positions, tiles, LANES), jnp.float32),
        ],
        compiler_params=pltpu.CompilerParams(vmem_limit_bytes=VMEM_LIMIT),
        cost_estimate=pl.CostEstimate(flops=10_000_000_000, bytes_accessed=40_000_000, transcendentals=0),
    )(grad_normed, hat, rstd, x, vectors)


def swap(values, bit, devices):
    pairs = [(d, d ^ (1 << bit)) for d in range(devices)]
    return lax.ppermute(values, AXES, pairs)


def halve_start(current, left, bit, narrow, devices, index):
    columns = current.shape[-1]
    axis = left.index(bit)
    mine = (index >> bit) & 1
    kept = lax.dynamic_index_in_dim(current, mine, axis, keepdims=False)
    sent = lax.dynamic_index_in_dim(current, 1 - mine, axis, keepdims=False)
    if bit in narrow:
        sent = sent.astype(jnp.bfloat16)
    arrived = swap(sent.reshape(-1, columns), bit, devices).reshape(sent.shape)
    return kept + arrived.astype(jnp.float32), left[:axis] + left[axis + 1 :]


def exchange_kernel(
    devices, n_slide, sums_ref, pooled_ref, grad_ref, head_ref,
    total_ref, all_pooled_ref, all_grad_ref, all_head_ref, landed, send_sem, recv_sem,
):
    n_enc = devices // n_slide
    my_enc, my_slide = lax.axis_index("enc"), lax.axis_index("slide")
    me = my_enc * n_slide + my_slide

    def slot_of(device):
        return lax.rem(device, n_slide) * n_enc + device // n_slide

    def place(device):
        return {"enc": device // n_slide, "slide": lax.rem(device, n_slide)}

    def each(body):
        def step(k, carry):
            body(k, lax.rem(me + k, devices), lax.rem(me + devices - k, devices))
            return carry

        lax.fori_loop(1, devices, step, 0)

    def copy(kind, k, source, target, device):
        return pltpu.make_async_remote_copy(
            src_ref=source, dst_ref=target, send_sem=send_sem.at[kind, k],
            recv_sem=recv_sem.at[kind, k], device_id=place(device),
            device_id_type=pl.DeviceIdType.MESH,
        )

    barrier = pltpu.get_barrier_semaphore()
    each(lambda k, to, source: pl.semaphore_signal(
        barrier, inc=1, device_id=place(to), device_id_type=pl.DeviceIdType.MESH))
    pl.semaphore_wait(barrier, devices - 1)

    def sums(k, to, slot):
        return copy(0, k, sums_ref.at[to], landed.at[slot], to)

    def pooled(k, to, slot):
        return copy(1, k, pooled_ref.at[to], all_pooled_ref.at[slot], to)

    def spread(k, to, slot):
        device = to * n_slide + my_slide
        return (
            copy(2, k, grad_ref, all_grad_ref.at[my_slide, slot], device),
            copy(3, k, head_ref, all_head_ref.at[my_slide, slot], device),
        )

    def each_enc(body):
        def step(k, carry):
            body(k, lax.rem(my_enc + k, n_enc), lax.rem(my_enc + n_enc - k, n_enc))
            return carry

        lax.fori_loop(1, n_enc, step, 0)

    def flip(value, bit):
        return value + (1 << bit) * (1 - 2 * lax.rem(value // (1 << bit), 2))

    def passed(bit, held, first, receive):
        peer = flip(my_slide, bit)
        items = []
        for q, mask in enumerate(held):
            slot = peer if receive else my_slide
            for m in mask:
                slot = flip(slot, m)
            for kind, ref in ((2, all_grad_ref), (3, all_head_ref)):
                items.append(copy(
                    kind, n_enc + first + q, ref.at[slot], ref.at[slot],
                    my_enc * n_slide + peer))
        return items

    def totals(k, to, slot):
        return copy(4, k, total_ref.at[me], total_ref.at[slot], to)

    each(lambda k, to, source: sums(k, to, me).start())
    landed[me] = sums_ref[me]
    all_pooled_ref[slot_of(me)] = pooled_ref[me]
    all_grad_ref[my_slide, my_enc] = grad_ref[...]
    all_head_ref[my_slide, my_enc] = head_ref[...]

    def start_spread(k, to, source):
        for item in spread(k, to, my_enc):
            item.start()

    def wait_spread(k, to, source):
        for item in spread(k, to, source):
            item.wait_recv()

    def sent_spread(k, to, source):
        for item in spread(k, to, my_enc):
            item.wait_send()

    each_enc(start_spread)
    each(lambda k, to, source: pooled(k, to, slot_of(me)).start())
    each(lambda k, to, source: sums(k, to, source).wait_recv())
    total_ref[me] = jnp.sum(landed[...], axis=0)
    each(lambda k, to, source: totals(k, to, me).start())
    each_enc(wait_spread)
    held, first = [()], 0
    sent = []
    for bit in range(n_slide.bit_length() - 2, -1, -1):
        outgoing = passed(bit, held, first, False)
        for item in outgoing:
            item.start()
        sent += outgoing
        for item in passed(bit, held, first, True):
            item.wait_recv()
        first += len(held)
        held = held + [mask + (bit,) for mask in held]
    for item in sent:
        item.wait_send()
    each_enc(sent_spread)

    def finish(k, to, source):
        sums(k, to, me).wait_send()
        pooled(k, to, slot_of(source)).wait_recv()
        pooled(k, to, slot_of(me)).wait_send()
        totals(k, to, source).wait_recv()
        totals(k, to, me).wait_send()

    each(finish)


def exchange(devices, n_slide, sums, pooled, grad, head):
    return pl.pallas_call(
        partial(exchange_kernel, devices, n_slide),
        out_shape=(
            jax.ShapeDtypeStruct(sums.shape, sums.dtype),
            jax.ShapeDtypeStruct(pooled.shape, pooled.dtype),
            jax.ShapeDtypeStruct((n_slide, devices // n_slide) + grad.shape, grad.dtype),
            jax.ShapeDtypeStruct((n_slide, devices // n_slide) + head.shape, head.dtype),
        ),
        in_specs=whole_vmem(4),
        out_specs=tuple(whole_vmem(4)),
        scratch_shapes=[
            pltpu.VMEM(sums.shape, sums.dtype),
            pltpu.SemaphoreType.DMA((5, devices)),
            pltpu.SemaphoreType.DMA((5, devices)),
        ],
        compiler_params=pltpu.CompilerParams(
            collective_id=0, has_side_effects=True, vmem_limit_bytes=VMEM_LIMIT
        ),
        cost_estimate=pl.CostEstimate(
            flops=10_000_000_000, bytes_accessed=80_000_000, transcendentals=0
        ),
    )(sums, pooled, grad, head)


def per_device(
    tile_features, tile_slide, slide_order, targets, dw_kernel, dw_bias, norm_gain, norm_bias,
    w_in, in_bias, w_out, out_bias, layer_scale, final_gain, final_bias, head_weight, head_bias,
):
    highest = lax.Precision.HIGHEST
    f32 = jnp.float32
    bf16 = jnp.bfloat16
    tiles, channels = tile_features.shape[0], tile_features.shape[-1]
    ff = w_in.shape[0]
    n_enc, n_slide = lax.axis_size("enc"), lax.axis_size("slide")
    devices = n_enc * n_slide
    slides = slide_order.shape[1]
    owned = slides // n_slide
    genes = targets.shape[-1]
    enc_index, slide_index = lax.axis_index("enc"), lax.axis_index("slide")
    index = enc_index * n_slide + slide_index

    hot = (tile_slide == slide_order).astype(f32)
    early = jnp.concatenate([targets.reshape(-1), jnp.sum(hot, axis=0)])
    early = jnp.pad(early, (0, -early.shape[0] % channels)).reshape(-1, channels)

    x = jnp.transpose(tile_features, (1, 2, 0, 3)).reshape(POSITIONS, tiles, channels)
    vectors = jnp.stack([dw_bias, norm_gain, norm_bias]).astype(f32)
    normed, hat, rstd, feature_sum = prepare(x, dw_kernel, vectors)
    pooled_active, slope = hidden_layer(normed, w_in, in_bias[None, :], tiles)
    high = lax.reduce_precision(pooled_active, 8, 7)
    both = jnp.concatenate([high, pooled_active - high], axis=0).astype(bf16)
    product = jnp.dot(both, w_out, preferred_element_type=f32)
    branch = (product[:tiles] + product[tiles:]) / POSITIONS + out_bias.astype(f32)
    scale = layer_scale.astype(f32)
    pooled = feature_sum / POSITIONS + scale * branch
    embedded, pull_norm = jax.vjp(
        layer_norm, pooled, final_gain.astype(f32), final_bias.astype(f32)
    )
    partial_sums = lax.dot_general(
        hot.astype(bf16), embedded.astype(bf16), (((0,), (0,)), ((), ())),
        preferred_element_type=f32,
    )
    group = lax.all_gather(jnp.concatenate([partial_sums, early], axis=0), "slide")
    early = group[:, slides:].reshape(n_slide, -1)
    all_targets = early[:, : owned * genes].reshape(slides, genes)
    counts = jnp.sum(early[:, owned * genes : owned * genes + slides], axis=0)
    divisor = jnp.maximum(counts, 1.0)[:, None]
    slide_mean = jnp.sum(group[:, :slides], axis=0) / divisor
    head_wide = head_weight.astype(f32)
    prediction = jnp.dot(
        slide_mean, head_wide, precision=highest, preferred_element_type=f32
    ) + head_bias.astype(f32)
    difference = prediction - all_targets
    losses = 0.5 * jnp.mean(difference * difference, axis=-1)
    slide_loss = lax.dynamic_slice_in_dim(losses, slide_index * owned, owned)
    grad_pred = difference / genes
    grad_mean = lax.dot_general(
        grad_pred, head_wide, (((1,), (1,)), ((), ())), precision=highest,
        preferred_element_type=f32,
    )
    slide_grad = (grad_mean / divisor).astype(bf16)
    grad_embed = jnp.dot(hot.astype(bf16), slide_grad, preferred_element_type=f32)
    grad_pooled, grad_fgain, grad_fbias = pull_norm(grad_embed)
    grad_scale = jnp.sum(grad_pooled * branch, axis=0)
    scaled = grad_pooled * scale
    grad_out_bias = jnp.sum(scaled, axis=0)
    grad_projected = (scaled / POSITIONS).astype(bf16)
    grad_active = lax.dot_general(
        grad_projected, w_out, (((1,), (1,)), ((), ())), preferred_element_type=f32
    )
    grad_hidden, first, second, grad_inner = grad_hidden_layer(slope, grad_active, normed)

    bits = devices.bit_length() - 1
    inner = n_slide.bit_length() - 1
    xs = list(range(1, inner))
    rest = list(range(inner, bits))
    narrow = (1, inner, inner + 1)
    orders = ([0] + xs + rest, [0] + rest[:1] + xs + rest[1:])
    current = [
        part.reshape((2,) * bits + (ff // devices, channels // 2)) for part in (first, second)
    ]
    left = [list(range(bits - 1, -1, -1))] * 2

    def stage(number):
        for part in range(2):
            current[part], left[part] = halve_start(
                current[part], left[part], orders[part][number], narrow, devices, index
            )

    stage(0)
    grad_normed = jnp.dot(grad_hidden, w_in, preferred_element_type=f32)
    grad_normed, current[0], current[1] = lax.optimization_barrier(
        (grad_normed, current[0], current[1])
    )
    stage(1)
    small = prepare_back(grad_normed, hat, rstd, x, vectors)
    small, current[0], current[1] = lax.optimization_barrier((small, current[0], current[1]))
    stage(2)
    bundle = jnp.concatenate(
        [
            small, grad_out_bias[None], grad_scale[None], grad_fgain[None], grad_fbias[None],
            grad_inner.reshape(-1, channels),
        ],
        axis=0,
    )
    used = bundle.shape[0]
    bundle = jnp.pad(bundle, ((0, -used % devices), (0, 0))).reshape(devices, -1, channels)
    mine = pooled_active.reshape(tiles, devices, ff // devices).transpose(1, 0, 2)
    head_rows = lax.dynamic_slice_in_dim(
        jnp.concatenate([slide_mean, grad_pred], axis=1), slide_index * owned, owned
    )
    bundle, mine, all_grad, head_parts = exchange(
        devices, n_slide, bundle, mine, grad_projected, head_rows
    )
    bundle, mine, all_grad, head_parts, current[0], current[1] = lax.optimization_barrier(
        (bundle, mine, all_grad, head_parts, current[0], current[1])
    )
    for number in range(3, bits):
        stage(number)
    grad_w_in = jnp.concatenate(current, axis=1)
    bundle = bundle.reshape(-1, channels)
    head_parts = head_parts.reshape(-1, channels + genes)
    grad_head_w = lax.dot_general(
        head_parts[:, :channels], head_parts[:, channels:], (((0,), (0,)), ((), ())),
        precision=highest, preferred_element_type=f32,
    )
    grad_head_b = jnp.sum(head_parts[:, channels:], axis=0)
    mine = mine.reshape(devices * tiles, ff // devices)
    mine_high = lax.reduce_precision(mine, 8, 7)
    all_grad = all_grad.reshape(devices * tiles, channels)

    def rows_product(left):
        return lax.dot_general(
            left.astype(bf16), all_grad, (((0,), (0,)), ((), ())), preferred_element_type=f32
        )

    grad_w_out = rows_product(mine_high) + rows_product(mine - mine_high)
    taps = POSITIONS
    return (
        grad_w_in,
        grad_w_out,
        bundle[:taps],
        bundle[taps : taps + 7],
        bundle[taps + 7 : used].reshape(-1),
        grad_head_w,
        grad_head_b,
        slide_loss[None, :],
    )


def solution(mesh):
    placed = (
        P(AXES, None, None, None),
        P(AXES, None),
        P("enc", None),
        P("enc", "slide", None),
    ) + (P(),) * 13
    return jax.shard_map(
        per_device,
        mesh=mesh,
        in_specs=placed,
        out_specs=(P(AXES, None), P(AXES, None), P(), P(), P(), P(), P(), P("enc", "slide")),
        check_vma=False,
    )
```
